32 devices in a mesh: corpus: 4 (over z), rerank: 8 (over y, x, core).
Axes of the slice: x: 2, y: 2, z: 4, core: 2. Of those that a mesh axis runs over, the one named last changes fastest.
Arguments:
- store_rows: bfloat16 [128, 512, 3584], P('corpus', 'rerank'), may hold values from -400 to 400
- block_lengths: int32 [128], replicated, may hold values from 128 to 512
- queries: bfloat16 [32, 64, 3584], P(None, 'rerank'), may hold values from -400 to 400
- cand_owner: int32 [64, 1], replicated, may hold values from 0 to 3; in each aligned block of 16 rows (0 to 15, 16 to 31, ...) at most 5 rows name the same one
- cand_block: int32 [64], replicated, may hold values from 0 to 31
- cand_query: int32 [64], replicated, may hold values from 0 to 31
- norm_gain: bfloat16 [3584], replicated, may hold values from 0.099609375 to 1.8984375
- w_query: bfloat16 [3584, 1792], P('rerank'), may hold values from -8 to 8
- w_key: bfloat16 [3584, 256], P('rerank'), may hold values from -1 to 1
- w_value: bfloat16 [3584, 256], P('rerank'), may hold values from -0.09375 to 0.09375
- w_score: bfloat16 [1792], replicated, may hold values from -0.125 to 0.125
Outputs:
- passage_context: bfloat16 [80, 512, 1792], P('corpus', 'rerank')
- pair_scores: float32 [64], P(('corpus', 'rerank'))
The draws below stay inside these ranges and needn't reach their ends.
Inputs may be any that keep to these rules, and one draw needn't show every extreme that they name: `cand_owner`: at most 5 of the 16 pairs of one corpus group (an aligned block of rows) name the same owner, in every draw, some group names one owner in exactly 5 of its 16 pairs.
All inputs are finite; a program needn't handle non-finite values.
Results may differ from the reference program's by a relative error of at most 0.013.
Values may be sent and summed in bfloat16 or wider, within the bound.
A program may use at most 128 MiB of HBM per device.

```python
import math
import jax
import jax.numpy as jnp
import numpy as np
from jax import lax

D = 3584
HDIM = 128
QHEADS = 14
KVHEADS = 2
QW = 1792
KW = 256
BLK = 512
QLEN = 64
CAP = 5
PAIR_C = 16
PAIRS = 64
OWN_BLKS = 32
NQ = 32
BLOCKS = 128
N_CORPUS = 4


def hidden_rows(key, shape):
    noise_key = jax.random.fold_in(key, 3)
    column_key = jax.random.fold_in(key, 5)
    row_key = jax.random.fold_in(key, 7)
    base = jax.random.truncated_normal(noise_key, -4.0, 4.0, shape, jnp.float32)
    columns = jnp.exp(jax.random.uniform(column_key, (shape[-1],), jnp.float32, 0.0, math.log(10.0)))
    row_scale = jnp.exp(jax.random.uniform(row_key, shape[:-1] + (1,), jnp.float32, 0.0, math.log(10.0)))
    return jnp.clip(base * columns * row_scale, -400.0, 400.0)


def draw_store_rows(key, part):
    return hidden_rows(jax.random.fold_in(key, 101), (BLOCKS, BLK, D)).astype(jnp.bfloat16)


def draw_queries(key, part):
    return hidden_rows(jax.random.fold_in(key, 202), (NQ, QLEN, D)).astype(jnp.bfloat16)


def key_matrix(key):
    return jax.random.truncated_normal(jax.random.fold_in(key, 11), -4.0, 4.0, (D, KVHEADS * HDIM), jnp.float32) * D ** (-0.5)


def draw_w_key(key, part):
    return key_matrix(key).astype(jnp.bfloat16)


def draw_w_query(key, part):
    noise = jax.random.truncated_normal(jax.random.fold_in(key, 23), -4.0, 4.0, (D, QHEADS * HDIM), jnp.float32) * D ** (-0.5)
    return noise.astype(jnp.bfloat16)


def plant(array, rng, least, high):
    spot = [jax.random.randint(jax.random.fold_in(rng, axis), (), 0, length) for axis, length in enumerate(array.shape)]
    widest = array.shape.index(max(array.shape))
    beside = spot[:widest] + [(spot[widest] + 1) % array.shape[widest]] + spot[widest + 1:]
    return array.at[tuple(spot)].set(least).at[tuple(beside)].set(high)


def block_levels(own_key, dims, cuts, smallest, largest):
    def one(position, blocks):
        heights = jax.random.uniform(jax.random.fold_in(jax.random.fold_in(own_key, 6), position), (blocks,), jnp.float32, smallest / len(cuts), largest / len(cuts))
        return jnp.repeat(jnp.exp(heights), dims[position] // blocks).reshape((-1,) + (1,) * (len(dims) - position - 1))

    factor_of = one(*cuts[0])
    for cut in cuts[1:]:
        factor_of = factor_of * one(*cut)
    return factor_of


def deal_out(own_key, own, number, rows, count, top, bound, slope):
    ranking = jax.random.permutation(own_key, count)
    heavy_load, usual = load_shares(count, rows * top, bound, slope, True), load_shares(count, rows * top, bound, slope, False)
    places = jnp.arange(count)

    def named(lengths, turn):
        used = int((lengths > 0).sum())
        fixed = max(1, used // 4)
        passed = fixed + (places - fixed + turn * (used - fixed)) % max(1, count - fixed)
        return jnp.zeros((count,), jnp.int32).at[ranking[jnp.where(places < fixed, places, passed)]].set(jnp.asarray(lengths, jnp.int32))

    lengths = jnp.where(number % 4 == 0, named(heavy_load, number // 4), named(usual, number - number // 4 - 1))
    mixed = jax.random.permutation(jax.random.fold_in(own, 3), count)
    donor, taker = mixed[0:count // 2 * 2:2], mixed[1:count // 2 * 2:2]
    margin = jnp.minimum(lengths[donor] - 1, bound - lengths[taker]) // 2
    margin = jnp.where((donor == ranking[0]) | (taker == ranking[0]) | (lengths[taker] == 0), 0, jnp.maximum(margin, 0))
    passed = jax.random.randint(jax.random.fold_in(own, 4), (count // 2,), 0, 1 << 20) % (margin + 1)
    lengths = lengths.at[donor].add(-passed).at[taker].add(passed)
    labels = jnp.searchsorted(jnp.cumsum(lengths), jnp.arange(rows * top), side="right").astype(jnp.int32)
    listing = labels.reshape(top, rows).T
    listing = listing[jax.random.permutation(jax.random.fold_in(own, 1), rows)]
    turn = jax.random.randint(jax.random.fold_in(own, 2), (rows, 1), 0, top)
    return jnp.take_along_axis(listing, (jnp.arange(top)[None, :] + turn) % top, axis=1)


def load_shares(number_of, total, reach, lean, full):
    loads = [(1 << 20) // math.isqrt(standing ** lean) + 1 for standing in range(1, number_of + 1)]
    largest = reach if full else min(reach, max(-(-total // number_of), total * loads[0] // sum(loads)))
    least = 1 if total - largest >= number_of - 1 else 0
    counts, rest = [largest] + [least] * (number_of - 1), total - largest - least * (number_of - 1)
    while rest > 0:
        free = [i for i in range(1, number_of) if counts[i] < largest] or [i for i in range(1, number_of) if counts[i] < reach]
        mass, budget = sum([loads[i] for i in free]), rest
        for i in free:
            addition = min(reach - counts[i], max(1, budget * loads[i] // mass), rest)
            counts[i] = counts[i] + addition
            rest = rest - addition
    return np.array(counts)


def gaussian(key, dims, deviation, reach, split=(), kind=jnp.bfloat16):
    result = jax.random.normal(key, dims, jnp.float32) * deviation
    if len(split) > 0:
        result = block_levels(key, dims, split, -0.22, 0.18) * result
    return jnp.clip(result, min=-reach, max=reach).astype(kind)


def setup_inputs(seed: int = 0) -> dict:
    seeds = jax.random.split(jax.random.key(seed), 12)
    store_rows = draw_store_rows(jax.random.fold_in(seeds[11], 71), 0)
    block_lengths = plant(jax.random.randint(seeds[1], (BLOCKS,), BLK // 4, BLK + 1), jax.random.fold_in(seeds[1], 1), BLK // 4, BLK).astype(jnp.int32)
    queries = draw_queries(jax.random.fold_in(seeds[11], 71), 0)
    cand_owner_keys = jax.random.split(jax.random.fold_in(seeds[3], 1), PAIRS // PAIR_C)
    cand_owner_turns = jax.random.permutation(jax.random.fold_in(seeds[3], 3), PAIRS // PAIR_C)
    cand_owner = jax.vmap(lambda own, number: deal_out(jax.random.fold_in(seeds[3], 2), own, number, PAIR_C, N_CORPUS, 1, CAP, 2))(cand_owner_keys, cand_owner_turns).reshape((PAIRS, 1))
    cand_block = plant(jax.random.randint(seeds[4], (PAIRS,), 0, OWN_BLKS), jax.random.fold_in(seeds[4], 1), 0, OWN_BLKS - 1).astype(jnp.int32)
    cand_query = plant(jax.random.randint(seeds[5], (PAIRS,), 0, NQ), jax.random.fold_in(seeds[5], 1), 0, NQ - 1).astype(jnp.int32)
    norm_gain = jnp.clip(1.0 + 0.18 * jax.random.normal(seeds[6], (D,), jnp.float32), 0.099609375, 1.8984375).astype(jnp.bfloat16)
    w_query = draw_w_query(jax.random.fold_in(seeds[11], 71), 0)
    w_key = draw_w_key(jax.random.fold_in(seeds[11], 71), 0)
    w_value = gaussian(seeds[9], (D, KW), D ** -0.5, 0.09375, ((0, 8),))
    w_score = gaussian(seeds[10], (QW,), QW ** -0.5, 0.125)
    return {"store_rows": store_rows, "block_lengths": block_lengths, "queries": queries, "cand_owner": cand_owner, "cand_block": cand_block, "cand_query": cand_query, "norm_gain": norm_gain, "w_query": w_query, "w_key": w_key, "w_value": w_value, "w_score": w_score}


ROPE_BASE = 1000000.0
EPSILON = 1e-06

def rotate(values, positions):
    head_dim = values.shape[-1]
    half_dim = head_dim // 2
    inverse = jnp.power(ROPE_BASE, -2.0 * jnp.arange(half_dim, dtype=jnp.float32) / head_dim)
    angles = positions.astype(jnp.float32)[..., None] * inverse
    cosine = jnp.cos(angles)[..., None, :]
    sine_part = jnp.sin(angles)[..., None, :]
    lower = values[..., :half_dim]
    upper = values[..., half_dim:]
    return jnp.concatenate([lower * cosine - upper * sine_part, upper * cosine + lower * sine_part], axis=-1)

def attend(joined, length, norm_gain, w_query, w_key, w_value, w_score):
    seq_len = joined.shape[0]
    widened = joined.astype(jnp.float32)
    inverse_rms = lax.rsqrt(lax.optimization_barrier(jnp.mean(widened * widened, axis=-1, keepdims=True)) + EPSILON)
    normed = (widened * inverse_rms * norm_gain.astype(jnp.float32)).astype(jnp.bfloat16)
    query_raw = jnp.dot(normed, w_query, preferred_element_type=jnp.float32)
    key_raw = jnp.dot(normed, w_key, preferred_element_type=jnp.float32)
    value_raw = jnp.dot(normed, w_value, preferred_element_type=jnp.float32)
    token_ids = jnp.arange(seq_len, dtype=jnp.int32)
    positions = jnp.where(token_ids < BLK, token_ids, length + token_ids - BLK)
    query_rot = rotate(query_raw.reshape(seq_len, QHEADS, HDIM), positions).astype(jnp.bfloat16)
    key_rot = rotate(key_raw.reshape(seq_len, KVHEADS, HDIM), positions).astype(jnp.bfloat16)
    values = value_raw.reshape(seq_len, KVHEADS, HDIM).astype(jnp.bfloat16)
    grouped = query_rot.reshape(seq_len, KVHEADS, QHEADS // KVHEADS, HDIM)
    logits = jnp.einsum('skgd,tkd->kgst', grouped.astype(jnp.float32), key_rot.astype(jnp.float32)) * HDIM ** (-0.5)
    live = (token_ids < length) | (token_ids >= BLK)
    allowed = live[None, :] & (token_ids[None, :] <= token_ids[:, None])
    masked = jnp.where(allowed, logits, -1e+30)
    peak = lax.optimization_barrier(jnp.max(masked, axis=-1, keepdims=True))
    weights = jnp.where(allowed, jnp.exp(masked - peak), 0.0)
    probs = (weights / lax.optimization_barrier(jnp.sum(weights, axis=-1, keepdims=True))).astype(jnp.bfloat16)
    context = jnp.einsum('kgst,tkd->skgd', probs.astype(jnp.float32), values.astype(jnp.float32))
    context = context.reshape(seq_len, QHEADS * HDIM).astype(jnp.bfloat16)
    score = jnp.dot(context[seq_len - 1], w_score, preferred_element_type=jnp.float32)
    keep = token_ids[:BLK] < length
    passage = jnp.where(keep[:, None], context[:BLK], jnp.zeros((), jnp.bfloat16))
    return (passage, score)

def reference(store_rows, block_lengths, queries, cand_owner, cand_block, cand_query, norm_gain, w_query, w_key, w_value, w_score):
    pair_total = cand_block.shape[0]
    pair_group = pair_total // N_CORPUS
    owners = cand_owner[:, 0]
    pair_order = jnp.arange(pair_total, dtype=jnp.int32)
    group_of = pair_order // pair_group
    earlier = (owners[:, None] == owners[None, :]) & (group_of[:, None] == group_of[None, :]) & (pair_order[None, :] < pair_order[:, None])
    owner_rank = lax.optimization_barrier(jnp.sum(earlier.astype(jnp.int32), axis=1))
    block_of = owners * OWN_BLKS + cand_block

    def run_pair(index):
        block = block_of[index]
        joined = jnp.concatenate([store_rows[block], queries[cand_query[index]]], axis=0)
        return attend(joined, block_lengths[block], norm_gain, w_query, w_key, w_value, w_score)
    passages, pair_scores = lax.map(run_pair, pair_order)
    slot_ids = ((owners * N_CORPUS + group_of) * CAP + owner_rank).astype(jnp.int32)
    passage_context = jnp.zeros((N_CORPUS * N_CORPUS * CAP, BLK, QHEADS * HDIM), jnp.bfloat16).at[slot_ids].set(passages)
    return (passage_context, pair_scores)
```

```python
import functools

import jax
import jax.numpy as jnp
from jax import lax
from jax.experimental import pallas as pl
from jax.experimental.pallas import tpu as pltpu
from jax.sharding import PartitionSpec as P

HDIM = 128
QHEADS = 14
KVHEADS = 2
GROUP = QHEADS // KVHEADS
CAP = 5

ROPE_BASE = 1000000.0
EPSILON = 1e-06
NEG = -1e30
VMEM = 62 << 20


MESH = pl.DeviceIdType.MESH
WIDE = 2 * HDIM


def split_rows(rows, parts):
    unit = 16
    tiles = rows // unit
    sizes = [(tiles // parts + (p < tiles % parts)) * unit for p in range(parts)]
    starts = [sum(sizes[:p]) for p in range(parts)]
    return list(zip(starts, sizes))


def gather_project_kernel(
    plan,
    ids_ref,
    store_hbm,
    ask_ref,
    tail_hbm,
    gain_ref,
    wk_hbm,
    wv_hbm,
    wq_hbm,
    pcos_ref,
    psin_ref,
    acos_ref,
    asin_ref,
    out_hbm,
    kv_hbm,
    store,
    normed,
    weight,
    tail_raw,
    result,
    load_sem,
    own_sem,
    put_sem,
    tail_sem,
    send_sem,
    recv_sem,
):
    bits, slots, pieces, key_blocks, pair_blocks, blocks = plan
    member = lax.axis_index("rerank")
    links = list(range(1, bits))
    orders = [links[p:] + links[:p] for p in range(len(links))]
    stages = len(links)
    own_rows = wq_hbm.shape[0]
    chunk = store.shape[1]
    depth = store.shape[2]
    held = slots * chunk
    tail_rows = tail_raw.shape[0]
    total = normed.shape[0]
    piece_rows = held // pieces
    ask_rows = total - held - tail_rows

    def digit(b):
        return lax.rem(member // (2**b), 2)

    def across(b):
        return member + (1 - 2 * digit(b)) * (2**b)

    def place(spread):
        return tuple(slice(None) if b in spread else digit(b) for b in reversed(range(bits)))

    barrier = pltpu.get_barrier_semaphore()
    for b in range(bits):
        pl.semaphore_signal(
            barrier, inc=1, device_id={"rerank": across(b)}, device_id_type=MESH
        )

    own_copies = []
    for j in range(blocks):
        if j < key_blocks:
            source, column = wk_hbm, j
        elif j < pair_blocks:
            source, column = wv_hbm, j - key_blocks
        else:
            source, column = wq_hbm, j - pair_blocks
        own_copies.append(
            pltpu.make_async_copy(
                source.at[:, column * WIDE : (column + 1) * WIDE],
                weight.at[(j,) + place(())],
                own_sem.at[j],
            )
        )
        own_copies[-1].start()
    quarter = store.shape[0] // 4
    loads = [
        pltpu.make_async_copy(
            store_hbm.at[pl.ds(q * quarter, quarter)],
            store.at[pl.ds(q * quarter, quarter)],
            load_sem.at[q],
        )
        for q in range(4)
    ]
    for copy in loads:
        copy.start()
    pl.semaphore_wait(barrier, bits)

    wparts = split_rows(own_rows, stages)
    kparts = split_rows(piece_rows, stages)

    def link_copy(pairs, block, s, p):
        order = orders[p]
        if pairs:
            first, size = kparts[p]
            index = (block,) + place(order[:s]) + (slice(None), pl.ds(first, size))
            ref, at = kv_hbm, block + blocks
        else:
            first, size = wparts[p]
            index = (block,) + place(order[:s]) + (pl.ds(first, size),)
            ref, at = weight, block
        return pltpu.make_async_remote_copy(
            src_ref=ref.at[index],
            dst_ref=ref.at[index],
            send_sem=send_sem.at[at, s, p],
            recv_sem=recv_sem.at[at, s, p],
            device_id={"rerank": across(order[s])},
            device_id_type=MESH,
        )

    def core_copy(pairs, block):
        ref, at = (kv_hbm, block + blocks) if pairs else (weight, block)
        index = (block,) + place(links)
        return pltpu.make_async_remote_copy(
            src_ref=ref.at[index],
            dst_ref=ref.at[index],
            send_sem=send_sem.at[at, stages, 0],
            recv_sem=recv_sem.at[at, stages, 0],
            device_id={"rerank": across(0)},
            device_id_type=MESH,
        )

    def own_pairs(piece):
        return pltpu.make_async_copy(
            result.at[pl.ds(0, pair_blocks), pl.ds(pl.multiple_of(piece * piece_rows, 16), piece_rows)],
            kv_hbm.at[(piece,) + place(())],
            put_sem.at[piece + blocks],
        )

    def out_copy(block):
        return pltpu.make_async_copy(result.at[block], out_hbm.at[block], put_sem.at[block])

    def event(pairs, e, block):
        if e == 0 and pairs:
            own_pairs(block).wait()
        if 0 < e <= stages:
            for p in range(stages):
                link_copy(pairs, block, e - 1, p).wait_recv()
        if e < stages:
            for p in range(stages):
                link_copy(pairs, block, e, p).start()
        if e == stages:
            core_copy(pairs, block).start()
        if e == stages + 1:
            core_copy(pairs, block).wait_recv()

    def tail_copy(b):
        return pltpu.make_async_remote_copy(
            src_ref=tail_raw,
            dst_ref=tail_raw,
            send_sem=tail_sem.at[1 + b],
            recv_sem=tail_sem.at[0],
            device_id={"rerank": across(b)},
            device_id_type=MESH,
        )

    gain = gain_ref[...].astype(jnp.float32)

    def scaled(rows):
        rows = rows.astype(jnp.float32)
        scale = lax.rsqrt(jnp.mean(rows * rows, axis=-1, keepdims=True) + EPSILON)
        return (rows * scale * gain).astype(normed.dtype)

    strip = 16

    def norm_slots(lo, hi):
        @pl.loop(lo, hi)
        def _(s):
            block = ids_ref[s]
            for r in range(chunk // strip):
                row = pl.multiple_of(s * chunk + r * strip, strip)
                normed[pl.ds(row, strip), :] = scaled(store[block, r * strip : (r + 1) * strip, :])

    for copy in own_copies:
        copy.wait()
    lead = stages + 1
    cuts = [slots * i // lead for i in range(lead + 1)]
    last = 2**bits - 1

    @pl.when(member == last)
    def _():
        copy = pltpu.make_async_copy(tail_hbm, tail_raw, tail_sem.at[1 + bits])
        copy.start()
        copy.wait()

    for i in range(-lead, 0):
        for e in range(lead):
            block = i + lead - e
            if block >= 0:
                event(False, e, block)
        if i == -lead:
            for b in range(bits):
                top = 2 ** (bits - b) - 1
                if b > 0:

                    @pl.when(member // (2 ** (b - 1)) == 2 * top)
                    def _():
                        tail_copy(b - 1).wait_recv()

                @pl.when(member // (2**b) == top)
                def _():
                    tail_copy(b).start()

            @pl.loop(0, ask_rows // strip)
            def _(r):
                row = pl.multiple_of(r * strip, strip)
                normed[pl.ds(held + tail_rows + row, strip), :] = scaled(ask_ref[pl.ds(row, strip), :])

            for copy in loads:
                copy.wait()
        norm_slots(cuts[i + lead], cuts[i + lead + 1])

    @pl.when(member // (2 ** (bits - 1)) == 0)
    def _():
        tail_copy(bits - 1).wait_recv()

    for r in range(tail_rows // strip):
        normed[held + r * strip : held + (r + 1) * strip, :] = scaled(
            tail_raw[r * strip : (r + 1) * strip, :]
        )

    repeat = piece_rows // chunk

    def piece(block, start, rows, tail):
        x = normed[pl.ds(start, rows), :]
        w = weight[block].reshape(own_rows * 2**bits, WIDE)
        raw = jnp.dot(x, w, preferred_element_type=jnp.float32)
        plain = (block >= key_blocks) & (block < pair_blocks)

        def turn(part, cosine, sine):
            cosine = jnp.where(plain, 1.0, cosine)
            sine = jnp.where(plain, 0.0, sine)
            return part * cosine + pltpu.roll(part, HDIM // 2, 1) * sine

        for head in range(WIDE // HDIM):
            columns = slice(head * HDIM, (head + 1) * HDIM)
            for r in range(repeat):
                part = raw[r * chunk : (r + 1) * chunk, columns]
                result[block, pl.ds(start + r * chunk, chunk), columns] = turn(
                    part, pcos_ref[...], psin_ref[...]
                ).astype(result.dtype)
            if tail:
                result[block, held : held + tail, columns] = turn(
                    raw[piece_rows:, columns], acos_ref[:tail, :], asin_ref[:tail, :]
                ).astype(result.dtype)

    @pl.loop(0, blocks + pieces)
    def _(i):
        for e in range(lead + 1):
            block = i + lead - e

            @pl.when(block < blocks)
            def _():
                event(False, e, block)

            @pl.when((block >= blocks) & (block < blocks + pieces))
            def _():
                event(True, e, block - blocks)

        @pl.when(i < blocks)
        def _():
            @pl.loop(0, pieces - 1)
            def _(t):
                piece(i, pl.multiple_of(t * piece_rows, 16), piece_rows, 0)

        @pl.when(i < pair_blocks)
        def _():
            piece(i, held - piece_rows, piece_rows + tail_rows + ask_rows, tail_rows + ask_rows)

        @pl.when((i >= pair_blocks) & (i < blocks))
        def _():
            piece(i, held - piece_rows, piece_rows + tail_rows, tail_rows)

        @pl.when(i < blocks)
        def _():
            out_copy(i).start()

        @pl.when(i == pair_blocks - 1)
        def _():
            for p in range(pieces):
                own_pairs(p).start()

    @pl.loop(0, blocks)
    def _(j):
        out_copy(j).wait()
        for s in range(stages):
            for p in range(stages):
                link_copy(False, j, s, p).wait_send()
        core_copy(False, j).wait_send()

    @pl.loop(0, pieces)
    def _(j):
        for s in range(stages):
            for p in range(stages):
                link_copy(True, j, s, p).wait_send()
        core_copy(True, j).wait_send()

    for b in range(bits):

        @pl.when(member // (2**b) == 2 ** (bits - b) - 1)
        def _():
            tail_copy(b).wait_send()


def gather_project(ids, store, ask, tail, gain, wk, wv, wq, tables, bits, pieces):
    slots = ids.shape[0]
    _, chunk, depth = store.shape
    own_rows = wq.shape[0]
    key_blocks = wk.shape[1] // WIDE
    pair_blocks = key_blocks + wv.shape[1] // WIDE
    blocks = pair_blocks + wq.shape[1] // WIDE
    held = slots * chunk
    total = held + tail.shape[0] + ask.shape[0]
    piece_rows = held // pieces
    stages = bits - 1
    cube = (2,) * bits
    plan = (bits, slots, pieces, key_blocks, pair_blocks, blocks)
    whole = pl.BlockSpec(memory_space=pltpu.VMEM)
    apart = pl.BlockSpec(memory_space=pl.ANY)
    return pl.pallas_call(
        functools.partial(gather_project_kernel, plan),
        out_shape=(
            jax.ShapeDtypeStruct((blocks, total, WIDE), store.dtype),
            jax.ShapeDtypeStruct((pieces,) + cube + (pair_blocks, piece_rows, WIDE), store.dtype),
        ),
        in_specs=[
            pl.BlockSpec(memory_space=pltpu.SMEM),
            apart,
            whole,
            apart,
            whole,
            apart,
            apart,
            apart,
            whole,
            whole,
            whole,
            whole,
        ],
        out_specs=(apart, apart),
        scratch_shapes=[
            pltpu.VMEM(store.shape, store.dtype),
            pltpu.VMEM((total, depth), store.dtype),
            pltpu.VMEM((blocks,) + cube + (own_rows, WIDE), store.dtype),
            pltpu.VMEM(tail.shape, store.dtype),
            pltpu.VMEM((blocks, total, WIDE), store.dtype),
            pltpu.SemaphoreType.DMA((4,)),
            pltpu.SemaphoreType.DMA((blocks,)),
            pltpu.SemaphoreType.DMA((blocks + pieces,)),
            pltpu.SemaphoreType.DMA((bits + 2,)),
            pltpu.SemaphoreType.DMA((blocks + pieces, stages + 1, stages)),
            pltpu.SemaphoreType.DMA((blocks + pieces, stages + 1, stages)),
        ],
        compiler_params=pltpu.CompilerParams(
            vmem_limit_bytes=VMEM, collective_id=0, has_side_effects=True
        ),
        cost_estimate=pl.CostEstimate(
            flops=2 * total * depth * blocks * WIDE,
            transcendentals=0,
            bytes_accessed=2 * (total * depth + depth * blocks * WIDE),
        ),
    )(ids, store, ask, tail, gain, wk, wv, wq, *tables)


def attend_kernel(widths, len_ref, q_ref, kv_ref, out_ref):
    slot = pl.program_id(0)
    member = lax.axis_index("rerank")
    length = len_ref[slot]
    chunk = q_ref.shape[1]
    start = member * chunk
    live = start < length
    pair_blocks = kv_ref.shape[2]
    key_blocks = pair_blocks // 2
    scale = HDIM ** (-0.5)

    def spot(head):
        column = head * HDIM
        return column // WIDE, slice(column % WIDE, column % WIDE + HDIM)

    def attend(width):
        rows = GROUP * chunk
        token = start + lax.broadcasted_iota(jnp.int32, (chunk, width), 0)
        allowed = lax.broadcasted_iota(jnp.int32, (chunk, width), 1) <= token
        allowed = jnp.concatenate([allowed.astype(jnp.float32)] * GROUP, axis=0) > 0.5
        keep = start + lax.broadcasted_iota(jnp.int32, (chunk, HDIM), 0) < length
        for head in range(KVHEADS):
            parts = []
            for g in range(GROUP):
                block, columns = spot(head * GROUP + g)
                parts.append(q_ref[pair_blocks + block, :, columns])
            query = jnp.concatenate(parts, axis=0)
            block, columns = spot(head)
            key = kv_ref[0, : width // chunk, block, :, columns].reshape(width, HDIM)
            value = kv_ref[0, : width // chunk, key_blocks + block, :, columns].reshape(width, HDIM)
            logits = scale * lax.dot_general(
                query, key, (((1,), (1,)), ((), ())), preferred_element_type=jnp.float32
            )
            masked = jnp.where(allowed, logits, NEG)
            weights = jnp.exp(masked - jnp.max(masked, axis=-1, keepdims=True))
            inverse = 1.0 / jnp.sum(weights, axis=-1, keepdims=True)
            probs = (weights * inverse).astype(jnp.bfloat16)
            context = jnp.dot(probs, value, preferred_element_type=jnp.float32)
            for g in range(GROUP):
                part = context[g * chunk : (g + 1) * chunk]
                column = (head * GROUP + g) * HDIM
                out_ref[0, :, column : column + HDIM] = jnp.where(keep, part, 0.0).astype(
                    out_ref.dtype
                )

    @pl.when(jnp.logical_not(live))
    def _():
        out_ref[...] = jnp.zeros_like(out_ref)

    below = 0
    for width in widths:
        end = start + chunk

        @pl.when(live & (end > below) & (end <= width))
        def _(width=width):
            attend(width)

        below = width


def attend(lengths, chunk, projected, gathered):
    slots = lengths.shape[0]
    pieces, members, pair_blocks, piece_rows, _ = gathered.shape
    blocks = projected.shape[0]
    width = (blocks - pair_blocks) * WIDE
    tokens = members * chunk
    each = piece_rows // chunk
    widths = [w for w in (128, 256) if w < tokens and w % chunk == 0] + [tokens]
    return pl.pallas_call(
        functools.partial(attend_kernel, widths),
        out_shape=jax.ShapeDtypeStruct((slots, chunk, width), projected.dtype),
        grid_spec=pltpu.PrefetchScalarGridSpec(
            num_scalar_prefetch=1,
            grid=(slots,),
            in_specs=[
                pl.BlockSpec((blocks, chunk, WIDE), lambda s, n: (0, s, 0)),
                pl.BlockSpec(
                    (1, members, pair_blocks, chunk, WIDE),
                    lambda s, n: (s // each, 0, 0, s % each, 0),
                ),
            ],
            out_specs=pl.BlockSpec((1, chunk, width), lambda s, n: (s, 0, 0)),
        ),
        compiler_params=pltpu.CompilerParams(vmem_limit_bytes=48 << 20),
        cost_estimate=pl.CostEstimate(
            flops=4 * slots * chunk * tokens * width,
            transcendentals=slots * chunk * QHEADS * tokens,
            bytes_accessed=2 * slots * (2 * chunk * width + tokens * pair_blocks * WIDE),
        ),
    )(lengths, projected, gathered)


def last_token(query, passage, question, alive, w_score):
    slots = query.shape[0]
    heads = query.reshape(slots, KVHEADS, GROUP, HDIM)
    both = jnp.concatenate([passage, question], axis=1)
    both = both.reshape(slots, both.shape[1], 2, KVHEADS, HDIM)
    logits = jnp.einsum(
        "skgd,stkd->skgt", heads, both[:, :, 0], preferred_element_type=jnp.float32
    ) * HDIM ** (-0.5)
    masked = jnp.where(alive[:, None, None, :], logits, NEG)
    peak = jnp.max(masked, axis=-1)
    weights = jnp.exp(masked - peak[..., None])
    total = jnp.sum(weights, axis=-1)
    context = jnp.einsum(
        "skgt,stkd->skgd",
        weights.astype(jnp.bfloat16),
        both[:, :, 1],
        preferred_element_type=jnp.float32,
    )
    gains = w_score.astype(jnp.float32).reshape(KVHEADS, GROUP, HDIM)
    part = jnp.sum(context * gains[None], axis=-1)
    return tuple(v.reshape(slots, QHEADS) for v in (peak, total, part))


def on_device(
    store_rows,
    block_lengths,
    queries,
    cand_owner,
    cand_block,
    cand_query,
    norm_gain,
    w_query,
    w_key,
    w_value,
    w_score,
):
    n_corpus = lax.axis_size("corpus")
    n_rerank = lax.axis_size("rerank")
    corpus_index = lax.axis_index("corpus")
    member = lax.axis_index("rerank")
    pair_columns = w_key.shape[1] + w_value.shape[1]

    pair_total = cand_block.shape[0]
    pair_group = pair_total // n_corpus
    pair_dev = pair_group // n_rerank
    own_blocks, chunk, depth = store_rows.shape
    asking = queries.shape[1]
    owners = cand_owner[:, 0]
    pair_order = jnp.arange(pair_total, dtype=jnp.int32)
    group_of = pair_order // pair_group
    earlier = (
        (owners[:, None] == owners[None, :])
        & (group_of[:, None] == group_of[None, :])
        & (pair_order[None, :] < pair_order[:, None])
    )
    owner_rank = jnp.sum(earlier.astype(jnp.int32), axis=1)
    slots = n_corpus * CAP
    slot_ids = jnp.arange(slots, dtype=jnp.int32)
    wanted = (owners == corpus_index)[None, :] & (
        (group_of * CAP + owner_rank)[None, :] == slot_ids[:, None]
    )

    def per_slot(values):
        return jnp.sum(jnp.where(wanted, values[None, :], 0), axis=1)

    block_ids = per_slot(cand_block)
    query_ids = per_slot(cand_query)
    own_lengths = lax.dynamic_slice(block_lengths, (corpus_index * own_blocks,), (own_blocks,))
    chosen = block_ids[:, None] == jnp.arange(own_blocks, dtype=jnp.int32)[None, :]
    lengths = jnp.sum(jnp.where(chosen, own_lengths[None, :], 0), axis=1)
    lengths = jnp.where(jnp.any(wanted, axis=1), lengths, 0)

    gain = norm_gain[None, :]
    held = slots * chunk
    ask = jnp.take(queries, query_ids, axis=0).reshape(slots * asking, depth)
    tail = jnp.take(queries.reshape(-1, depth), query_ids * asking + asking - 1, axis=0)
    tail_rows = pl.cdiv(slots, 16) * 16
    tail = jnp.pad(tail, ((0, tail_rows - slots), (0, 0)))
    ends = jnp.pad(lengths + (n_rerank * asking - 1), (0, tail_rows - slots))
    here = member * chunk + jnp.arange(chunk, dtype=jnp.int32)
    there = lengths[:, None] + (member * asking + jnp.arange(asking, dtype=jnp.int32))[None, :]
    positions = jnp.concatenate([here, ends, there.reshape(-1)])
    half = HDIM // 2
    inverse = jnp.power(ROPE_BASE, -2.0 * jnp.arange(half, dtype=jnp.float32) / HDIM)
    angles = positions.astype(jnp.float32)[:, None] * inverse
    cosine = jnp.cos(angles)
    sine = jnp.sin(angles)
    cosine = jnp.concatenate([cosine, cosine], axis=1)
    sine = jnp.concatenate([-sine, sine], axis=1)
    tables = (cosine[:chunk], sine[:chunk], cosine[chunk:], sine[chunk:])
    bits = n_rerank.bit_length() - 1
    projected, gathered = gather_project(
        block_ids, store_rows, ask, tail, gain, w_key, w_value, w_query, tables, bits, n_corpus
    )
    pair_blocks = pair_columns // WIDE
    gathered = gathered.reshape((n_corpus, n_rerank) + gathered.shape[-3:])

    def side_by_side(values):
        return jnp.concatenate([values[i] for i in range(values.shape[0])], axis=1)

    tail_out = side_by_side(projected[pair_blocks:, held : held + slots])
    pair_out = side_by_side(projected[:pair_blocks, :held])
    ask_out = side_by_side(projected[:pair_blocks, held + tail_rows :])
    seen = (member * chunk + jnp.arange(chunk, dtype=jnp.int32))[None, :] < lengths[:, None]
    alive = jnp.concatenate([seen, jnp.ones((slots, asking), jnp.bool_)], axis=1)
    peak, total, part = last_token(
        tail_out,
        pair_out.reshape(slots, chunk, pair_columns),
        ask_out.reshape(slots, asking, pair_columns),
        alive,
        w_score,
    )

    def per_pair(values, absent):
        picked = jnp.sum(jnp.where(wanted[:, :, None], values[:, None, :], 0.0), axis=0)
        return jnp.where((owners == corpus_index)[:, None], picked, absent)

    mine = jnp.concatenate(
        [per_pair(peak, NEG), per_pair(total, 0.0), per_pair(part, 0.0)], axis=1
    )
    sources = n_corpus * n_rerank
    pieces = lax.all_to_all(
        mine.reshape(sources, pair_dev * 3 * QHEADS),
        ("corpus", "rerank"),
        split_axis=0,
        concat_axis=0,
        tiled=True,
    ).reshape(sources, pair_dev, 3, QHEADS)
    peak, total, part = pieces[:, :, 0], pieces[:, :, 1], pieces[:, :, 2]
    share = jnp.exp(peak - jnp.max(peak, axis=0, keepdims=True))
    ratio = jnp.sum(share * part, axis=0) / jnp.sum(share * total, axis=0)
    scores = jnp.sum(ratio, axis=-1)
    projected, scores = lax.optimization_barrier((projected, scores))
    context = attend(lengths, chunk, projected, gathered)
    return (context, scores)


def solution(mesh):
    placed = (
        P("corpus", "rerank", None),
        P(),
        P(None, "rerank", None),
        P(),
        P(),
        P(),
        P(),
        P("rerank", None),
        P("rerank", None),
        P("rerank", None),
        P(),
    )
    return jax.shard_map(
        on_device,
        mesh=mesh,
        in_specs=placed,
        out_specs=(P("corpus", "rerank", None), P(("corpus", "rerank"))),
        check_vma=False,
    )
```

```python
import functools

import jax
import jax.numpy as jnp
from jax import lax
from jax.experimental import pallas as pl
from jax.experimental.pallas import tpu as pltpu
from jax.sharding import PartitionSpec as P

HDIM = 128
QHEADS = 14
KVHEADS = 2
GROUP = QHEADS // KVHEADS
CAP = 5

ROPE_BASE = 1000000.0
EPSILON = 1e-06
NEG = -1e30
VMEM = 67043328


MESH = pl.DeviceIdType.MESH
WIDE = 2 * HDIM
DIRECT = 68


def split_rows(rows, parts):
    unit = 16
    tiles = rows // unit
    sizes = [(tiles // parts + (p < tiles % parts)) * unit for p in range(parts)]
    starts = [sum(sizes[:p]) for p in range(parts)]
    return list(zip(starts, sizes))


def gather_project_kernel(
    plan,
    ids_ref,
    len_ref,
    store_hbm,
    ask_hbm,
    tail_hbm,
    gain_ref,
    wk_hbm,
    wv_hbm,
    wq_hbm,
    pcos_ref,
    psin_ref,
    acos_ref,
    asin_ref,
    gains_ref,
    out_hbm,
    stat_hbm,
    store,
    normed,
    weight,
    tail_raw,
    result,
    pairs,
    stat,
    stat_in,
    load_sem,
    own_sem,
    put_sem,
    tail_sem,
    send_sem,
    recv_sem,
    out_sem,
    stat_sem,
):
    bits, slots, pieces, key_blocks, pair_blocks, blocks, n_corpus = plan
    member = lax.axis_index("rerank")
    corpus = lax.axis_index("corpus")
    shared = n_corpus % 2 == 0
    side = lax.rem(corpus, 2) if shared else 0
    mate = corpus + 1 - 2 * side
    links = list(range(1, bits))
    orders = [links[p:] + links[:p] for p in range(len(links))]
    stages = len(links)
    own_rows = wq_hbm.shape[0]
    chunk = store.shape[1]
    depth = store.shape[2]
    held = slots * chunk
    tail_rows = tail_raw.shape[0]
    total = normed.shape[0]
    piece_rows = held // pieces
    ask_rows = total - held - tail_rows

    def digit(b):
        return lax.rem(member // (2**b), 2)

    def across(b):
        return member + (1 - 2 * digit(b)) * (2**b)

    def place(spread):
        return tuple(slice(None) if b in spread else digit(b) for b in reversed(range(bits)))

    barrier = pltpu.get_barrier_semaphore()
    for b in range(bits):
        pl.semaphore_signal(
            barrier, inc=1, device_id={"rerank": across(b)}, device_id_type=MESH
        )
    for step in range(1, n_corpus):
        pl.semaphore_signal(
            barrier,
            inc=1,
            device_id={"corpus": lax.rem(corpus + step, n_corpus)},
            device_id_type=MESH,
        )

    own_copies = []
    for j in range(blocks):
        if j < key_blocks:
            source, column = wk_hbm, j
        elif j < pair_blocks:
            source, column = wv_hbm, j - key_blocks
        else:
            source, column = wq_hbm, j - pair_blocks
        own_copies.append(
            pltpu.make_async_copy(
                source.at[:, column * WIDE : (column + 1) * WIDE],
                weight.at[(j,) + place(())],
                own_sem.at[j],
            )
        )
        own_copies[-1].start()
    quarter = store.shape[0] // 4
    loads = [
        pltpu.make_async_copy(
            store_hbm.at[pl.ds(q * quarter, quarter)],
            store.at[pl.ds(q * quarter, quarter)],
            load_sem.at[q],
        )
        for q in range(4)
    ]
    loads.append(
        pltpu.make_async_copy(
            ask_hbm, normed.at[held + tail_rows :], load_sem.at[4]
        )
    )
    for copy in loads:
        copy.start()
    pl.semaphore_wait(barrier, bits + n_corpus - 1)

    own_units = own_rows // 16
    direct = (own_units * DIRECT // 100) * 16 if shared else own_rows
    traded = own_rows - direct
    wparts = split_rows(direct, stages)
    kparts = split_rows(piece_rows, stages)

    def remote(ref, index, at, s, p, device):
        return pltpu.make_async_remote_copy(
            src_ref=ref.at[index],
            dst_ref=ref.at[index],
            send_sem=send_sem.at[at, s, p],
            recv_sem=recv_sem.at[at, s, p],
            device_id=device,
            device_id_type=MESH,
        )

    def weight_copies(block, s):
        out = []
        if s < stages:
            for p in range(stages):
                first, size = wparts[p]
                rows = pl.ds(pl.multiple_of(side * traded + first, 16), size)
                index = (block,) + place(orders[p][:s]) + (rows,)
                device = {"rerank": across(orders[p][s])}
                out.append(remote(weight, index, block, s, p, device))
        elif shared and s == stages:
            rows = pl.ds(pl.multiple_of(side * direct, 16), traded)
            for p in range(stages):
                spots = list(place(links[p + 1 :]))
                spots[bits - 1 - links[p]] = 1 - digit(links[p])
                index = (block,) + tuple(spots) + (rows,)
                out.append(remote(weight, index, block, s, p, {"corpus": mate}))
        else:
            index = (block,) + place(links)
            out.append(remote(weight, index, block, stages + 1, 0, {"rerank": across(0)}))
        return out

    def pair_copies(piece, s):
        out = []
        at = piece + blocks
        if s < stages:
            for p in range(stages):
                first, size = kparts[p]
                index = (piece,) + place(orders[p][:s]) + (slice(None), pl.ds(first, size))
                out.append(remote(pairs, index, at, s, p, {"rerank": across(orders[p][s])}))
        else:
            index = (piece,) + place(links)
            out.append(remote(pairs, index, at, stages + 1, 0, {"rerank": across(0)}))
        return out

    weight_steps = stages + 1 + shared
    pair_steps = stages + 1

    def own_pairs(piece):
        first = pl.multiple_of(piece * piece_rows, 16)
        return pltpu.make_async_copy(
            result.at[pl.ds(0, pair_blocks), pl.ds(first, piece_rows)],
            pairs.at[(piece,) + place(())],
            put_sem.at[piece],
        )

    def own_weight(block):
        return pltpu.make_async_copy(
            wq_hbm.at[:, :WIDE], weight.at[(block,) + place(())], own_sem.at[block]
        )

    def weight_event(e, block):
        if e == 0:
            own_weight(block).wait()
        else:
            for copy in weight_copies(block, e - 1):
                copy.wait_recv()
        if e < weight_steps:
            for copy in weight_copies(block, e):
                copy.start()

    def pair_event(e, piece):
        if e == 0:
            own_pairs(piece).wait()
        else:
            for copy in pair_copies(piece, e - 1):
                copy.wait_recv()
        if e < pair_steps:
            for copy in pair_copies(piece, e):
                copy.start()

    tail_order = links + [0]

    def ones(order):
        value = 1
        for b in order:
            value = value * digit(b)
        return value

    def tail_gets(t):
        return ones(tail_order[t + 1 :]) * (1 - digit(tail_order[t])) == 1

    def tail_gives(t):
        return ones(tail_order[t:]) == 1

    def tail_copy(t):
        return pltpu.make_async_remote_copy(
            src_ref=tail_raw,
            dst_ref=tail_raw,
            send_sem=tail_sem.at[1 + t],
            recv_sem=tail_sem.at[0],
            device_id={"rerank": across(tail_order[t])},
            device_id_type=MESH,
        )

    gain = gain_ref[...].astype(jnp.float32)

    def scaled(rows):
        rows = rows.astype(jnp.float32)
        scale = lax.rsqrt(jnp.mean(rows * rows, axis=-1, keepdims=True) + EPSILON)
        return (rows * scale * gain).astype(normed.dtype)

    strip = 16

    def norm_slots(lo, hi):
        @pl.loop(lo, hi)
        def _(s):
            block = ids_ref[s]
            for r in range(chunk // strip):
                row = pl.multiple_of(s * chunk + r * strip, strip)
                normed[pl.ds(row, strip), :] = scaled(store[block, r * strip : (r + 1) * strip, :])

    lead = weight_steps
    cuts = [slots * i // lead for i in range(lead + 1)]

    @pl.when(ones(tail_order) == 1)
    def _():
        copy = pltpu.make_async_copy(tail_hbm, tail_raw, tail_sem.at[1 + bits])
        copy.start()
        copy.wait()

    for i in range(-lead, 0):
        for e in range(lead):
            block = i + lead - e
            if block >= 0:
                weight_event(e, block)
        if i == -lead:
            for copy in loads:
                copy.wait()

            @pl.loop(0, ask_rows // strip)
            def _(r):
                rows = pl.ds(pl.multiple_of(held + tail_rows + r * strip, strip), strip)
                normed[rows, :] = scaled(normed[rows, :])

        norm_slots(cuts[i + lead], cuts[i + lead + 1])
        t = i + lead
        if t < bits:
            if t > 0:
                pl.when(tail_gets(t - 1))(lambda: tail_copy(t - 1).wait_recv())
            pl.when(tail_gives(t))(lambda: tail_copy(t).start())
    for t in range(min(lead, bits), bits):
        pl.when(tail_gets(t - 1))(lambda: tail_copy(t - 1).wait_recv())
        pl.when(tail_gives(t))(lambda: tail_copy(t).start())
    pl.when(tail_gets(bits - 1))(lambda: tail_copy(bits - 1).wait_recv())

    for r in range(tail_rows // strip):
        normed[held + r * strip : held + (r + 1) * strip, :] = scaled(
            tail_raw[r * strip : (r + 1) * strip, :]
        )

    repeat = piece_rows // chunk

    def piece(block, start, rows, tail):
        x = normed[pl.ds(start, rows), :]
        w = weight[block].reshape(own_rows * 2**bits, WIDE)
        raw = jnp.dot(x, w, preferred_element_type=jnp.float32)
        plain = (block >= key_blocks) & (block < pair_blocks)

        def turn(part, cosine, sine):
            cosine = jnp.where(plain, 1.0, cosine)
            sine = jnp.where(plain, 0.0, sine)
            return part * cosine + pltpu.roll(part, HDIM // 2, 1) * sine

        for head in range(WIDE // HDIM):
            columns = slice(head * HDIM, (head + 1) * HDIM)
            for r in range(repeat):
                part = raw[r * chunk : (r + 1) * chunk, columns]
                result[block, pl.ds(start + r * chunk, chunk), columns] = turn(
                    part, pcos_ref[...], psin_ref[...]
                ).astype(result.dtype)
            if tail:
                result[block, held : held + tail, columns] = turn(
                    raw[piece_rows:, columns], acos_ref[:tail, :], asin_ref[:tail, :]
                ).astype(result.dtype)

    each = piece_rows // chunk
    scale = HDIM ** (-0.5)
    lanes = stat.shape[2]
    used = GROUP * tail_rows

    def spot(head):
        column = head * HDIM
        return column // WIDE, slice(column % WIDE, column % WIDE + HDIM)

    def tail_stats():
        rows = []
        for head in range(KVHEADS):
            parts = []
            for g in range(GROUP):
                block, columns = spot(head * GROUP + g)
                parts.append(result[pair_blocks + block, held : held + tail_rows, columns])
            query = jnp.concatenate(parts, axis=0)
            block, columns = spot(head)

            def both(block):
                return jnp.concatenate(
                    [result[block, :held, columns], result[block, held + tail_rows :, columns]],
                    axis=0,
                )

            key, value = both(block), both(key_blocks + block)
            slot = lax.rem(lax.broadcasted_iota(jnp.int32, (chunk, used), 1), tail_rows)
            token = member * chunk + lax.broadcasted_iota(jnp.int32, (chunk, used), 0)
            asked = ask_rows // slots
            slot_asked = lax.rem(lax.broadcasted_iota(jnp.int32, (asked, used), 1), tail_rows)

            def logits_of(lo, hi):
                return scale * lax.dot_general(
                    key[lo:hi], query, (((1,), (1,)), ((), ())), preferred_element_type=jnp.float32
                )

            seen = jnp.full((chunk, used), NEG, jnp.float32)
            for p in range(pieces):
                logits = logits_of(p * piece_rows, (p + 1) * piece_rows)
                for u in range(each):
                    s = p * each + u
                    alive = (slot == s) & (token < len_ref[s])
                    seen = jnp.where(alive, logits[u * chunk : (u + 1) * chunk], seen)
            logits = logits_of(held, held + ask_rows)
            asks = jnp.full((asked, used), NEG, jnp.float32)
            for s in range(slots):
                asks = jnp.where(slot_asked == s, logits[s * asked : (s + 1) * asked], asks)
            peak = jnp.maximum(
                jnp.max(seen, axis=0, keepdims=True), jnp.max(asks, axis=0, keepdims=True)
            )
            seen = jnp.exp(seen - peak)
            asks = jnp.exp(asks - peak)
            total = jnp.sum(seen, axis=0, keepdims=True) + jnp.sum(asks, axis=0, keepdims=True)
            spread = [
                jnp.where(slot == s, seen, 0.0).astype(jnp.bfloat16) for s in range(slots)
            ]
            spread.append(
                jnp.concatenate(
                    [jnp.where(slot_asked == s, asks, 0.0) for s in range(slots)], axis=0
                ).astype(jnp.bfloat16)
            )
            weighed = lax.dot_general(
                gains_ref[...], value, (((1,), (1,)), ((), ())), preferred_element_type=jnp.float32
            )
            mixed = jnp.dot(
                weighed.astype(jnp.bfloat16),
                jnp.concatenate(spread, axis=0),
                preferred_element_type=jnp.float32,
            )
            which = lax.broadcasted_iota(jnp.int32, mixed.shape, 0)
            wanted = head * GROUP + lax.broadcasted_iota(jnp.int32, mixed.shape, 1) // tail_rows
            part = jnp.sum(jnp.where(which == wanted, mixed, 0.0), axis=0, keepdims=True)
            rows.append((peak, total, part))
        stat[0] = jnp.zeros((8, lanes), jnp.float32)
        for k in range(3):
            for head in range(KVHEADS):
                row = k * KVHEADS + head
                stat[0, row : row + 1, :used] = rows[head][k]

    def stat_copy(t):
        return pltpu.make_async_remote_copy(
            src_ref=stat.at[t],
            dst_ref=stat_in.at[t],
            send_sem=stat_sem.at[0, t],
            recv_sem=stat_sem.at[1, t],
            device_id={"rerank": across(t)},
            device_id_type=MESH,
        )

    def score_copy(step):
        return pltpu.make_async_remote_copy(
            src_ref=stat.at[bits],
            dst_ref=stat_hbm.at[corpus],
            send_sem=stat_sem.at[0, bits + step],
            recv_sem=stat_sem.at[1, bits + step],
            device_id={"corpus": lax.rem(corpus + step, n_corpus)},
            device_id_type=MESH,
        )

    def score_own():
        return pltpu.make_async_copy(
            stat.at[bits], stat_hbm.at[corpus], stat_sem.at[0, bits + n_corpus]
        )

    def merge_stats():
        for t in range(bits):
            stat_copy(t).start()
            stat_copy(t).wait_recv()
            mine, other = stat[t], stat_in[t]

            def rows(values, k):
                return values[k * KVHEADS : (k + 1) * KVHEADS]

            peak = jnp.maximum(rows(mine, 0), rows(other, 0))
            left = jnp.exp(rows(mine, 0) - peak)
            right = jnp.exp(rows(other, 0) - peak)
            stat[t + 1] = jnp.zeros((8, lanes), jnp.float32)
            stat[t + 1, :KVHEADS] = peak
            for k in (1, 2):
                stat[t + 1, k * KVHEADS : (k + 1) * KVHEADS] = left * rows(mine, k) + right * rows(
                    other, k
                )
        for step in range(1, n_corpus):
            score_copy(step).start()
        score_own().start()

    def attend_slot(p, u, t):
        width = chunk * 2**t
        rows = pl.ds(pl.multiple_of(p * piece_rows + u * chunk, chunk), chunk)
        inner = pl.ds(pl.multiple_of(u * chunk, chunk), chunk)
        corner = (p,) + (0,) * (bits - t) + (slice(None),) * t
        token = member * chunk + lax.broadcasted_iota(jnp.int32, (chunk, width), 0)
        allowed = lax.broadcasted_iota(jnp.int32, (chunk, width), 1) <= token
        for head in range(KVHEADS):
            spots = [spot(head * GROUP + g) for g in range(GROUP)]
            query = jnp.concatenate(
                [result[pair_blocks + block, rows, columns] for block, columns in spots], axis=0
            )
            block, columns = spot(head)
            key = pairs[corner + (block, inner, columns)].reshape(width, HDIM)
            value = pairs[corner + (key_blocks + block, inner, columns)].reshape(width, HDIM)
            logits = lax.dot_general(
                query, key, (((1,), (1,)), ((), ())), preferred_element_type=jnp.float32
            ).reshape(GROUP, chunk, width)
            masked = jnp.where(allowed[None], logits, NEG)
            peak = jnp.max(masked, axis=-1, keepdims=True)
            weights = jnp.exp(scale * (masked - peak))
            inverse = 1.0 / jnp.sum(weights, axis=-1, keepdims=True)
            context = jnp.dot(
                weights.reshape(GROUP * chunk, width).astype(jnp.bfloat16),
                value,
                preferred_element_type=jnp.float32,
            )
            context = context.reshape(GROUP, chunk, HDIM) * inverse
            for g, (block, columns) in enumerate(spots):
                result[pair_blocks + block, rows, columns] = context[g].astype(result.dtype)

    def context_copy(p, j):
        rows = pl.ds(pl.multiple_of(p * piece_rows, 16), piece_rows)
        return pltpu.make_async_copy(
            result.at[pair_blocks + j, rows],
            out_hbm.at[rows, j * WIDE : (j + 1) * WIDE],
            out_sem.at[p, j],
        )

    def attend_piece(p):
        reach = [t for t in range(bits) if chunk * 2**t >= HDIM] + [bits]
        for k, t in enumerate(reach):
            low = 0 if k == 0 else 2 ** reach[k - 1]

            @pl.when((member >= low) & (member < 2**t))
            def _():
                @pl.loop(0, each)
                def _(u):
                    attend_slot(p, u, t)

        for j in range(blocks - pair_blocks):
            context_copy(p, j).start()

    begin = max(blocks - pair_steps - 1, pair_blocks)
    finish = begin + pieces + pair_steps

    @pl.loop(0, finish)
    def _(i):
        for e in range(weight_steps + 1):
            block = i + lead - e

            @pl.when(block < blocks)
            def _():
                weight_event(e, block)

        for e in range(pair_steps + 1):
            place_of = i - begin - e

            @pl.when((place_of >= 0) & (place_of < pieces))
            def _():
                pair_event(e, place_of)

        @pl.when(i < blocks)
        def _():
            @pl.loop(0, pieces - 1)
            def _(t):
                piece(i, pl.multiple_of(t * piece_rows, 16), piece_rows, 0)

        @pl.when(i < pair_blocks)
        def _():
            piece(i, held - piece_rows, piece_rows + tail_rows + ask_rows, tail_rows + ask_rows)

        @pl.when((i >= pair_blocks) & (i < blocks))
        def _():
            piece(i, held - piece_rows, piece_rows + tail_rows, tail_rows)

        @pl.when(i == pair_blocks - 1)
        def _():
            for p in range(pieces):
                own_pairs(p).start()

        @pl.when(i == blocks - 1)
        def _():
            tail_stats()

        @pl.when(i == blocks)
        def _():
            merge_stats()

        done = i - begin - pair_steps

        @pl.when(done >= 0)
        def _():
            attend_piece(done)

    for step in range(1, n_corpus):
        score_copy(step).wait()
    score_own().wait()
    for t in range(bits):
        stat_copy(t).wait_send()

    @pl.loop(0, blocks)
    def _(j):
        for s in range(weight_steps):
            for copy in weight_copies(j, s):
                copy.wait_send()

    @pl.loop(0, pieces)
    def _(p):
        for s in range(pair_steps):
            for copy in pair_copies(p, s):
                copy.wait_send()
        for j in range(blocks - pair_blocks):
            context_copy(p, j).wait()

    for t in range(bits):
        pl.when(tail_gives(t))(lambda: tail_copy(t).wait_send())


def fused(ids, lengths, store, ask, tail, gain, wk, wv, wq, tables, gains, bits, n_corpus):
    slots = ids.shape[0]
    pieces = n_corpus
    _, chunk, depth = store.shape
    own_rows = wq.shape[0]
    key_blocks = wk.shape[1] // WIDE
    pair_blocks = key_blocks + wv.shape[1] // WIDE
    blocks = pair_blocks + wq.shape[1] // WIDE
    held = slots * chunk
    total = held + tail.shape[0] + ask.shape[0]
    piece_rows = held // pieces
    stages = bits - 1
    cube = (2,) * bits
    lanes = pl.cdiv(GROUP * tail.shape[0], 128) * 128
    plan = (bits, slots, pieces, key_blocks, pair_blocks, blocks, n_corpus)
    whole = pl.BlockSpec(memory_space=pltpu.VMEM)
    apart = pl.BlockSpec(memory_space=pl.ANY)
    scalar = pl.BlockSpec(memory_space=pltpu.SMEM)
    return pl.pallas_call(
        functools.partial(gather_project_kernel, plan),
        out_shape=(
            jax.ShapeDtypeStruct((held, wq.shape[1]), store.dtype),
            jax.ShapeDtypeStruct((n_corpus, 8, lanes), jnp.float32),
        ),
        in_specs=[scalar, scalar, apart, apart, apart, whole, apart, apart, apart]
        + [whole] * (len(tables) + 1),
        out_specs=(apart, apart),
        scratch_shapes=[
            pltpu.VMEM(store.shape, store.dtype),
            pltpu.VMEM((total, depth), store.dtype),
            pltpu.VMEM((blocks,) + cube + (own_rows, WIDE), store.dtype),
            pltpu.VMEM(tail.shape, store.dtype),
            pltpu.VMEM((blocks, total, WIDE), store.dtype),
            pltpu.VMEM((pieces,) + cube + (pair_blocks, piece_rows, WIDE), store.dtype),
            pltpu.VMEM((bits + 1, 8, lanes), jnp.float32),
            pltpu.VMEM((bits, 8, lanes), jnp.float32),
            pltpu.SemaphoreType.DMA((5,)),
            pltpu.SemaphoreType.DMA((blocks,)),
            pltpu.SemaphoreType.DMA((pieces,)),
            pltpu.SemaphoreType.DMA((bits + 2,)),
            pltpu.SemaphoreType.DMA((blocks + pieces, stages + 2, stages)),
            pltpu.SemaphoreType.DMA((blocks + pieces, stages + 2, stages)),
            pltpu.SemaphoreType.DMA((pieces, blocks - pair_blocks)),
            pltpu.SemaphoreType.DMA((2, bits + n_corpus + 1)),
        ],
        compiler_params=pltpu.CompilerParams(
            vmem_limit_bytes=VMEM, collective_id=0, has_side_effects=True
        ),
        cost_estimate=pl.CostEstimate(
            flops=2 * total * depth * blocks * WIDE,
            transcendentals=0,
            bytes_accessed=2 * (total * depth + depth * blocks * WIDE),
        ),
    )(ids, lengths, store, ask, tail, gain, wk, wv, wq, *tables, gains)


def on_device(
    store_rows,
    block_lengths,
    queries,
    cand_owner,
    cand_block,
    cand_query,
    norm_gain,
    w_query,
    w_key,
    w_value,
    w_score,
):
    n_corpus = lax.axis_size("corpus")
    n_rerank = lax.axis_size("rerank")
    corpus_index = lax.axis_index("corpus")
    member = lax.axis_index("rerank")

    pair_total = cand_block.shape[0]
    pair_group = pair_total // n_corpus
    pair_dev = pair_group // n_rerank
    own_blocks, chunk, depth = store_rows.shape
    asking = queries.shape[1]
    owners = cand_owner[:, 0]
    pair_order = jnp.arange(pair_total, dtype=jnp.int32)
    group_of = pair_order // pair_group
    earlier = (
        (owners[:, None] == owners[None, :])
        & (group_of[:, None] == group_of[None, :])
        & (pair_order[None, :] < pair_order[:, None])
    )
    owner_rank = jnp.sum(earlier.astype(jnp.int32), axis=1)
    slots = n_corpus * CAP
    slot_ids = jnp.arange(slots, dtype=jnp.int32)
    wanted = (owners == corpus_index)[None, :] & (
        (group_of * CAP + owner_rank)[None, :] == slot_ids[:, None]
    )

    def per_slot(values):
        return jnp.sum(jnp.where(wanted, values[None, :], 0), axis=1)

    block_ids = per_slot(cand_block)
    query_ids = per_slot(cand_query)
    own_lengths = lax.dynamic_slice(block_lengths, (corpus_index * own_blocks,), (own_blocks,))
    chosen = block_ids[:, None] == jnp.arange(own_blocks, dtype=jnp.int32)[None, :]
    lengths = jnp.sum(jnp.where(chosen, own_lengths[None, :], 0), axis=1)
    lengths = jnp.where(jnp.any(wanted, axis=1), lengths, 0)

    gain = norm_gain[None, :]
    held = slots * chunk
    ask = jnp.take(queries, query_ids, axis=0).reshape(slots * asking, depth)
    tail = jnp.take(queries.reshape(-1, depth), query_ids * asking + asking - 1, axis=0)
    tail_rows = pl.cdiv(slots, 16) * 16
    tail = jnp.pad(tail, ((0, tail_rows - slots), (0, 0)))
    ends = jnp.pad(lengths + (n_rerank * asking - 1), (0, tail_rows - slots))
    here = member * chunk + jnp.arange(chunk, dtype=jnp.int32)
    there = lengths[:, None] + (member * asking + jnp.arange(asking, dtype=jnp.int32))[None, :]
    positions = jnp.concatenate([here, ends, there.reshape(-1)])
    half = HDIM // 2
    inverse = jnp.power(ROPE_BASE, -2.0 * jnp.arange(half, dtype=jnp.float32) / HDIM)
    angles = positions.astype(jnp.float32)[:, None] * inverse
    cosine = jnp.cos(angles)
    sine = jnp.sin(angles)
    cosine = jnp.concatenate([cosine, cosine], axis=1)
    sine = jnp.concatenate([-sine, sine], axis=1)
    tables = (cosine[:chunk], sine[:chunk], cosine[chunk:], sine[chunk:])
    bits = n_rerank.bit_length() - 1
    gains = w_score.reshape(QHEADS, HDIM)
    context, stats = fused(
        block_ids,
        lengths,
        store_rows,
        ask,
        tail,
        gain,
        w_key,
        w_value,
        w_query,
        tables,
        gains,
        bits,
        n_corpus,
    )
    wide = context.shape[1]
    here = member * chunk + jnp.arange(chunk, dtype=jnp.int32)
    keep = here[None, :, None] < lengths[:, None, None]
    context = jnp.where(keep, context.reshape(slots, chunk, wide), 0)
    used = GROUP * tail_rows
    ratio = stats[:, 2 * KVHEADS : 3 * KVHEADS, :used] / stats[:, KVHEADS : 2 * KVHEADS, :used]
    ratio = ratio.reshape(n_corpus, KVHEADS * GROUP, tail_rows).sum(axis=1)[:, :slots]
    first = corpus_index * pair_group + member * pair_dev
    mine = first + jnp.arange(pair_dev, dtype=jnp.int32)
    is_mine = mine[:, None] == pair_order[None, :]

    def of_mine(values):
        return jnp.sum(jnp.where(is_mine, values[None, :], 0), axis=1)

    place = of_mine(owners) * slots + corpus_index * CAP + of_mine(owner_rank)
    spread = jnp.arange(n_corpus * slots, dtype=jnp.int32)
    scores = jnp.sum(
        jnp.where(place[:, None] == spread[None, :], ratio.reshape(1, -1), 0.0), axis=1
    )
    return (context, scores)


def solution(mesh):
    placed = (
        P("corpus", "rerank", None),
        P(),
        P(None, "rerank", None),
        P(),
        P(),
        P(),
        P(),
        P("rerank", None),
        P("rerank", None),
        P("rerank", None),
        P(),
    )
    return jax.shard_map(
        on_device,
        mesh=mesh,
        in_specs=placed,
        out_specs=(P("corpus", "rerank", None), P(("corpus", "rerank"))),
        check_vma=False,
    )
```

```python
import functools

import jax
import jax.numpy as jnp
from jax import lax
from jax.experimental import pallas as pl
from jax.experimental.pallas import tpu as pltpu
from jax.sharding import PartitionSpec as P

HDIM = 128
QHEADS = 14
KVHEADS = 2
GROUP = QHEADS // KVHEADS
CAP = 5

ROPE_BASE = 1000000.0
EPSILON = 1e-06
NEG = -1e30
VMEM = 67043328


MESH = pl.DeviceIdType.MESH
WIDE = 2 * HDIM
DIRECT = 68
AHEAD = 2
WAIT = 3


def split_rows(rows, parts):
    unit = 16
    tiles = rows // unit
    sizes = [(tiles // parts + (p < tiles % parts)) * unit for p in range(parts)]
    starts = [sum(sizes[:p]) for p in range(parts)]
    return list(zip(starts, sizes))


def gather_project_kernel(
    plan,
    owner_ref,
    pick_ref,
    ask_ref,
    length_ref,
    store_hbm,
    query_hbm,
    gain_ref,
    wk_hbm,
    wv_hbm,
    wq_hbm,
    inverse_ref,
    gains_ref,
    out_hbm,
    score_ref,
    ids_ref,
    len_ref,
    query_ids,
    store,
    queries,
    normed,
    weight,
    result,
    pairs,
    pcos_ref,
    psin_ref,
    acos_ref,
    asin_ref,
    stat,
    stat_in,
    stat_all,
    load_sem,
    own_sem,
    put_sem,
    tail_sem,
    send_sem,
    recv_sem,
    out_sem,
    stat_sem,
):
    bits, slots, pieces, tiles, key_blocks, pair_blocks, blocks, n_corpus = plan
    member = lax.axis_index("rerank")
    corpus = lax.axis_index("corpus")
    shared = n_corpus % 2 == 0
    side = lax.rem(corpus, 2) if shared else 0
    mate = corpus + 1 - 2 * side
    links = list(range(1, bits))
    orders = [links[p:] + links[:p] for p in range(len(links))]
    stages = len(links)
    own_rows = wq_hbm.shape[0]
    chunk = store.shape[1]
    depth = store.shape[2]
    held = slots * chunk
    total = normed.shape[0]
    tail_rows = pl.cdiv(slots, 16) * 16
    piece_rows = held // pieces
    ask_rows = total - held - tail_rows

    def digit(b):
        return lax.rem(member // (2**b), 2)

    def across(b):
        return member + (1 - 2 * digit(b)) * (2**b)

    def place(spread):
        return tuple(slice(None) if b in spread else digit(b) for b in reversed(range(bits)))

    barrier = pltpu.get_barrier_semaphore()
    for b in range(bits):
        pl.semaphore_signal(
            barrier, inc=1, device_id={"rerank": across(b)}, device_id_type=MESH
        )
    for step in range(1, n_corpus):
        pl.semaphore_signal(
            barrier,
            inc=1,
            device_id={"corpus": lax.rem(corpus + step, n_corpus)},
            device_id_type=MESH,
        )

    own_copies = []
    for j in range(blocks):
        if j < key_blocks:
            source, column = wk_hbm, j
        elif j < pair_blocks:
            source, column = wv_hbm, j - key_blocks
        else:
            source, column = wq_hbm, j - pair_blocks
        own_copies.append(
            pltpu.make_async_copy(
                source.at[:, column * WIDE : (column + 1) * WIDE],
                weight.at[(j,) + place(())],
                own_sem.at[j],
            )
        )
        own_copies[-1].start()
    quarter = store.shape[0] // 4
    loads = [
        pltpu.make_async_copy(
            store_hbm.at[pl.ds(q * quarter, quarter)],
            store.at[pl.ds(q * quarter, quarter)],
            load_sem.at[q],
        )
        for q in range(4)
    ]
    loads.append(pltpu.make_async_copy(query_hbm, queries, load_sem.at[4]))
    for copy in loads:
        copy.start()
    pair_group = owner_ref.shape[0] // n_corpus

    @pl.loop(0, n_corpus)
    def _(g):
        def look(q, carry):
            count, picks, asks = carry
            p = g * pair_group + q
            mine = owner_ref[p] == corpus
            picks = tuple(
                jnp.where(mine & (count == r), pick_ref[p], v) for r, v in enumerate(picks)
            )
            asks = tuple(jnp.where(mine & (count == r), ask_ref[p], v) for r, v in enumerate(asks))
            return count + jnp.where(mine, 1, 0), picks, asks

        none = (jnp.int32(0),) * CAP
        count, picks, asks = lax.fori_loop(0, pair_group, look, (jnp.int32(0), none, none))
        for r in range(CAP):
            ids_ref[g * CAP + r] = picks[r]
            query_ids[g * CAP + r] = asks[r]
            length = length_ref[corpus * store.shape[0] + picks[r]]
            len_ref[g * CAP + r] = jnp.where(count > r, length, 0)

    pl.semaphore_wait(barrier, bits + n_corpus - 1)

    own_units = own_rows // 16
    direct = (own_units * DIRECT // 100) * 16 if shared else own_rows
    traded = own_rows - direct
    wparts = split_rows(direct, stages)
    kparts = split_rows(piece_rows, stages)

    def remote(ref, index, at, s, p, device):
        return pltpu.make_async_remote_copy(
            src_ref=ref.at[index],
            dst_ref=ref.at[index],
            send_sem=send_sem.at[at, s, p],
            recv_sem=recv_sem.at[at, s, p],
            device_id=device,
            device_id_type=MESH,
        )

    def weight_copies(block, s):
        out = []
        if s < stages:
            for p in range(stages):
                first, size = wparts[p]
                rows = pl.ds(pl.multiple_of(side * traded + first, 16), size)
                index = (block,) + place(orders[p][:s]) + (rows,)
                device = {"rerank": across(orders[p][s])}
                out.append(remote(weight, index, block, s, p, device))
        elif shared and s == stages:
            rows = pl.ds(pl.multiple_of(side * direct, 16), traded)
            for p in range(stages):
                spots = list(place(links[p + 1 :]))
                spots[bits - 1 - links[p]] = 1 - digit(links[p])
                index = (block,) + tuple(spots) + (rows,)
                out.append(remote(weight, index, block, s, p, {"corpus": mate}))
        else:
            index = (block,) + place(links)
            out.append(remote(weight, index, block, stages + 1, 0, {"rerank": across(0)}))
        return out

    def pair_copies(piece, s):
        out = []
        at = piece + blocks
        if s < stages:
            for p in range(stages):
                first, size = kparts[p]
                index = (piece,) + place(orders[p][:s]) + (slice(None), pl.ds(first, size))
                out.append(remote(pairs, index, at, s, p, {"rerank": across(orders[p][s])}))
        else:
            index = (piece,) + place(links)
            out.append(remote(pairs, index, at, stages + 1, 0, {"rerank": across(0)}))
        return out

    weight_steps = stages + 1 + shared
    pair_steps = stages + 1

    def own_pairs(piece):
        first = pl.multiple_of(piece * piece_rows, 16)
        return pltpu.make_async_copy(
            result.at[pl.ds(0, pair_blocks), pl.ds(first, piece_rows)],
            pairs.at[(piece,) + place(())],
            put_sem.at[piece],
        )

    def own_weight(block):
        return pltpu.make_async_copy(
            wq_hbm.at[:, :WIDE], weight.at[(block,) + place(())], own_sem.at[block]
        )

    def weight_event(e, block):
        if e == 0:
            own_weight(block).wait()
        else:
            for copy in weight_copies(block, e - 1):
                copy.wait_recv()
        if e < weight_steps:
            for copy in weight_copies(block, e):
                copy.start()

    def pair_event(e, piece):
        if e == 0:
            own_pairs(piece).wait()
        else:
            for copy in pair_copies(piece, e - 1):
                copy.wait_recv()
        if e < pair_steps:
            for copy in pair_copies(piece, e):
                copy.start()

    tail_order = links + [0]

    def ones(order):
        value = 1
        for b in order:
            value = value * digit(b)
        return value

    def tail_gets(t):
        return ones(tail_order[t + 1 :]) * (1 - digit(tail_order[t])) == 1

    def tail_gives(t):
        return ones(tail_order[t:]) == 1

    def tail_copy(t):
        return pltpu.make_async_remote_copy(
            src_ref=normed.at[held : held + tail_rows],
            dst_ref=normed.at[held : held + tail_rows],
            send_sem=tail_sem.at[1 + t],
            recv_sem=tail_sem.at[0],
            device_id={"rerank": across(tail_order[t])},
            device_id_type=MESH,
        )

    gain = gain_ref[...].astype(jnp.float32).reshape(1, depth)

    def scaled(rows):
        rows = rows.astype(jnp.float32)
        scale = lax.rsqrt(jnp.mean(rows * rows, axis=-1, keepdims=True) + EPSILON)
        return (rows * scale * gain).astype(normed.dtype)

    strip = 16

    def norm_slots(lo, hi):
        @pl.loop(lo, hi)
        def _(s):
            block = ids_ref[s]
            for r in range(chunk // strip):
                row = pl.multiple_of(s * chunk + r * strip, strip)
                normed[pl.ds(row, strip), :] = scaled(store[block, r * strip : (r + 1) * strip, :])

    lead = weight_steps
    cuts = [slots * i // lead for i in range(lead + 1)]

    asking = queries.shape[1]

    def asked_rows(s):
        return queries[query_ids[s]].astype(jnp.float32)

    def tables():
        def turn(positions):
            angles = positions.astype(jnp.float32) * inverse_ref[...]
            lane = lax.broadcasted_iota(jnp.int32, angles.shape, 1)
            sine = jnp.sin(angles)
            return jnp.cos(angles), jnp.where(lane < HDIM // 2, -sine, sine)

        here = lax.broadcasted_iota(jnp.int32, (chunk, HDIM), 0)
        pcos_ref[...], psin_ref[...] = turn(member * chunk + here)
        row = lax.broadcasted_iota(jnp.int32, (tail_rows, HDIM), 0)
        ends = jnp.zeros((tail_rows, HDIM), jnp.int32)
        row_asked = lax.broadcasted_iota(jnp.int32, (ask_rows, HDIM), 0)
        starts = member * asking + lax.rem(row_asked, asking)
        for s in range(slots):
            ends = jnp.where(row == s, len_ref[s] + (asking * 2**bits - 1), ends)
            starts = starts + jnp.where(row_asked // asking == s, len_ref[s], 0)
        acos_ref[:tail_rows], asin_ref[:tail_rows] = turn(ends)
        acos_ref[tail_rows:], asin_ref[tail_rows:] = turn(starts)

    for block in range(AHEAD):
        weight_event(0, block)
    for i in range(-lead, 0):
        for e in range(lead):
            block = i + lead - e + (AHEAD if e == 0 else 0)
            if block >= 0:
                weight_event(e, block)
        if i == -lead:
            tables()
            for copy in loads:
                copy.wait()

            @pl.when(ones(tail_order) == 1)
            def _():
                for r in range(tail_rows // strip):
                    rows = []
                    for s in range(r * strip, (r + 1) * strip):
                        rows.append(asked_rows(min(s, slots - 1))[asking - 1 :])
                    normed[held + r * strip : held + (r + 1) * strip, :] = jnp.concatenate(
                        rows, axis=0
                    ).astype(normed.dtype)

            @pl.loop(0, ask_rows // strip)
            def _(r):
                rows = pl.ds(pl.multiple_of(held + tail_rows + r * strip, strip), strip)
                each = strip // asking
                normed[rows, :] = scaled(
                    jnp.concatenate([asked_rows(r * each + k) for k in range(each)], axis=0)
                )

        norm_slots(cuts[i + lead], cuts[i + lead + 1])
        t = i + lead
        if t < bits:
            if t > 0:
                pl.when(tail_gets(t - 1))(lambda: tail_copy(t - 1).wait_recv())
            pl.when(tail_gives(t))(lambda: tail_copy(t).start())
    for t in range(min(lead, bits), bits):
        pl.when(tail_gets(t - 1))(lambda: tail_copy(t - 1).wait_recv())
        pl.when(tail_gives(t))(lambda: tail_copy(t).start())
    pl.when(tail_gets(bits - 1))(lambda: tail_copy(bits - 1).wait_recv())

    for t in range(bits):
        pl.when(tail_gives(t))(lambda: tail_copy(t).wait_send())
    for r in range(tail_rows // strip):
        rows = slice(held + r * strip, held + (r + 1) * strip)
        normed[rows, :] = scaled(normed[rows, :])

    tile_rows = held // tiles
    repeat = tile_rows // chunk

    def piece(block, start, rows, tail):
        x = normed[pl.ds(start, rows), :]
        w = weight[block].reshape(own_rows * 2**bits, WIDE)
        raw = jnp.dot(x, w, preferred_element_type=jnp.float32)
        plain = (block >= key_blocks) & (block < pair_blocks)

        def turn(part, cosine, sine):
            cosine = jnp.where(plain, 1.0, cosine)
            sine = jnp.where(plain, 0.0, sine)
            return part * cosine + pltpu.roll(part, HDIM // 2, 1) * sine

        for head in range(WIDE // HDIM):
            columns = slice(head * HDIM, (head + 1) * HDIM)
            for r in range(repeat):
                part = raw[r * chunk : (r + 1) * chunk, columns]
                result[block, pl.ds(start + r * chunk, chunk), columns] = turn(
                    part, pcos_ref[...], psin_ref[...]
                ).astype(result.dtype)
            if tail:
                result[block, held : held + tail, columns] = turn(
                    raw[tile_rows:, columns], acos_ref[:tail, :], asin_ref[:tail, :]
                ).astype(result.dtype)

    each = piece_rows // chunk
    scale = HDIM ** (-0.5)
    lanes = stat.shape[2]
    used = GROUP * tail_rows

    def spot(head):
        column = head * HDIM
        return column // WIDE, slice(column % WIDE, column % WIDE + HDIM)

    def tail_stats():
        rows = []
        for head in range(KVHEADS):
            parts = []
            for g in range(GROUP):
                block, columns = spot(head * GROUP + g)
                parts.append(result[pair_blocks + block, held : held + tail_rows, columns])
            query = jnp.concatenate(parts, axis=0)
            block, columns = spot(head)

            def both(block):
                return jnp.concatenate(
                    [result[block, :held, columns], result[block, held + tail_rows :, columns]],
                    axis=0,
                )

            key, value = both(block), both(key_blocks + block)
            slot = lax.rem(lax.broadcasted_iota(jnp.int32, (chunk, used), 1), tail_rows)
            token = member * chunk + lax.broadcasted_iota(jnp.int32, (chunk, used), 0)
            asked = ask_rows // slots
            slot_asked = lax.rem(lax.broadcasted_iota(jnp.int32, (asked, used), 1), tail_rows)

            def logits_of(lo, hi):
                return scale * lax.dot_general(
                    key[lo:hi], query, (((1,), (1,)), ((), ())), preferred_element_type=jnp.float32
                )

            seen = jnp.full((chunk, used), NEG, jnp.float32)
            for p in range(tiles):
                logits = logits_of(p * tile_rows, (p + 1) * tile_rows)
                for u in range(repeat):
                    s = p * repeat + u
                    alive = (slot == s) & (token < len_ref[s])
                    seen = jnp.where(alive, logits[u * chunk : (u + 1) * chunk], seen)
            logits = logits_of(held, held + ask_rows)
            asks = jnp.full((asked, used), NEG, jnp.float32)
            for s in range(slots):
                asks = jnp.where(slot_asked == s, logits[s * asked : (s + 1) * asked], asks)
            peak = jnp.maximum(
                jnp.max(seen, axis=0, keepdims=True), jnp.max(asks, axis=0, keepdims=True)
            )
            seen = jnp.exp(seen - peak)
            asks = jnp.exp(asks - peak)
            total = jnp.sum(seen, axis=0, keepdims=True) + jnp.sum(asks, axis=0, keepdims=True)
            spread = [
                jnp.where(slot == s, seen, 0.0).astype(jnp.bfloat16) for s in range(slots)
            ]
            spread.append(
                jnp.concatenate(
                    [jnp.where(slot_asked == s, asks, 0.0) for s in range(slots)], axis=0
                ).astype(jnp.bfloat16)
            )
            weighed = lax.dot_general(
                gains_ref[...], value, (((1,), (1,)), ((), ())), preferred_element_type=jnp.float32
            )
            mixed = jnp.dot(
                weighed.astype(jnp.bfloat16),
                jnp.concatenate(spread, axis=0),
                preferred_element_type=jnp.float32,
            )
            which = lax.broadcasted_iota(jnp.int32, mixed.shape, 0)
            wanted = head * GROUP + lax.broadcasted_iota(jnp.int32, mixed.shape, 1) // tail_rows
            part = jnp.sum(jnp.where(which == wanted, mixed, 0.0), axis=0, keepdims=True)
            rows.append((peak, total, part))
        stat[0] = jnp.zeros((8, lanes), jnp.float32)
        for k in range(3):
            for head in range(KVHEADS):
                row = k * KVHEADS + head
                stat[0, row : row + 1, :used] = rows[head][k]

    def stat_copy(t):
        return pltpu.make_async_remote_copy(
            src_ref=stat.at[t],
            dst_ref=stat_in.at[t],
            send_sem=stat_sem.at[0, t],
            recv_sem=stat_sem.at[1, t],
            device_id={"rerank": across(t)},
            device_id_type=MESH,
        )

    def score_copy(step):
        return pltpu.make_async_remote_copy(
            src_ref=stat.at[bits],
            dst_ref=stat_all.at[corpus],
            send_sem=stat_sem.at[0, bits + step],
            recv_sem=stat_sem.at[1, bits + step],
            device_id={"corpus": lax.rem(corpus + step, n_corpus)},
            device_id_type=MESH,
        )

    def score_own():
        return pltpu.make_async_copy(
            stat.at[bits], stat_all.at[corpus], stat_sem.at[0, bits + n_corpus]
        )

    def merge_stats():
        for t in range(bits):
            stat_copy(t).start()
            stat_copy(t).wait_recv()
            mine, other = stat[t], stat_in[t]

            def rows(values, k):
                return values[k * KVHEADS : (k + 1) * KVHEADS]

            peak = jnp.maximum(rows(mine, 0), rows(other, 0))
            left = jnp.exp(rows(mine, 0) - peak)
            right = jnp.exp(rows(other, 0) - peak)
            stat[t + 1] = jnp.zeros((8, lanes), jnp.float32)
            stat[t + 1, :KVHEADS] = peak
            for k in (1, 2):
                stat[t + 1, k * KVHEADS : (k + 1) * KVHEADS] = left * rows(mine, k) + right * rows(
                    other, k
                )
        for step in range(1, n_corpus):
            score_copy(step).start()
        score_own().start()

    def attend_slot(p, u, t):
        width = chunk * 2**t
        rows = pl.ds(pl.multiple_of(p * piece_rows + u * chunk, chunk), chunk)
        inner = pl.ds(pl.multiple_of(u * chunk, chunk), chunk)
        corner = (p,) + (0,) * (bits - t) + (slice(None),) * t
        token = member * chunk + lax.broadcasted_iota(jnp.int32, (chunk, width), 0)
        allowed = lax.broadcasted_iota(jnp.int32, (chunk, width), 1) <= token
        keep = member * chunk + lax.broadcasted_iota(jnp.int32, (chunk, HDIM), 0)
        keep = keep < len_ref[p * each + u]
        for head in range(KVHEADS):
            spots = [spot(head * GROUP + g) for g in range(GROUP)]
            query = jnp.concatenate(
                [result[pair_blocks + block, rows, columns] for block, columns in spots], axis=0
            )
            block, columns = spot(head)
            key = pairs[corner + (block, inner, columns)].reshape(width, HDIM)
            value = pairs[corner + (key_blocks + block, inner, columns)].reshape(width, HDIM)
            logits = lax.dot_general(
                query, key, (((1,), (1,)), ((), ())), preferred_element_type=jnp.float32
            ).reshape(GROUP, chunk, width)
            masked = jnp.where(allowed[None], logits, NEG)
            peak = jnp.max(masked, axis=-1, keepdims=True)
            weights = jnp.exp(scale * (masked - peak))
            inverse = 1.0 / jnp.sum(weights, axis=-1, keepdims=True)
            context = jnp.dot(
                weights.reshape(GROUP * chunk, width).astype(jnp.bfloat16),
                value,
                preferred_element_type=jnp.float32,
            )
            context = context.reshape(GROUP, chunk, HDIM) * inverse
            for g, (block, columns) in enumerate(spots):
                result[pair_blocks + block, rows, columns] = jnp.where(
                    keep, context[g], 0.0
                ).astype(result.dtype)

    def context_copy(p, j):
        rows = pl.ds(pl.multiple_of(p * piece_rows, 16), piece_rows)
        return pltpu.make_async_copy(
            result.at[pair_blocks + j, rows],
            out_hbm.at[rows, j * WIDE : (j + 1) * WIDE],
            out_sem.at[p, j],
        )

    def attend_piece(p):
        reach = [t for t in range(bits) if chunk * 2**t >= HDIM] + [bits]
        for k, t in enumerate(reach):
            low = 0 if k == 0 else 2 ** reach[k - 1]

            @pl.when((member >= low) & (member < 2**t))
            def _():
                @pl.loop(0, each)
                def _(u):
                    attend_slot(p, u, t)

        for j in range(blocks - pair_blocks):
            context_copy(p, j).start()

    begin = pair_blocks + WAIT
    finish = max(begin + pair_steps, blocks) + pieces

    @pl.loop(0, finish)
    def _(i):
        for e in range(weight_steps + 1):
            block = i + lead - e + (AHEAD if e == 0 else 0)

            @pl.when(block < blocks)
            def _():
                weight_event(e, block)

            if e <= pair_steps:
                part = i - begin - e

                @pl.when((part >= 0) & (part < pieces))
                def _():
                    pair_event(e, part)

        @pl.when(i < blocks)
        def _():
            @pl.loop(0, tiles - 1)
            def _(t):
                piece(i, pl.multiple_of(t * tile_rows, 16), tile_rows, 0)

        @pl.when(i < pair_blocks)
        def _():
            piece(i, held - tile_rows, tile_rows + tail_rows + ask_rows, tail_rows + ask_rows)

        @pl.when((i >= pair_blocks) & (i < blocks))
        def _():
            piece(i, held - tile_rows, tile_rows + tail_rows, tail_rows)

        @pl.when(i == pair_blocks - 1)
        def _():
            for p in range(pieces):
                own_pairs(p).start()

        @pl.when(i == blocks - 1)
        def _():
            tail_stats()

        @pl.when(i == blocks)
        def _():
            merge_stats()

        late = max(begin + pair_steps, blocks)
        done = i - late

        @pl.when((done >= 0) & (done < pieces))
        def _():
            attend_piece(done)

    for step in range(1, n_corpus):
        score_copy(step).wait()
    score_own().wait()
    pair_dev = pair_group // 2**bits
    first = corpus * pair_group
    for d in range(pair_dev):
        own = member * pair_dev + d
        name = owner_ref[first + own]

        def count(q, value):
            return value + jnp.where((owner_ref[first + q] == name) & (q < own), 1, 0)

        slot = corpus * CAP + lax.fori_loop(0, pair_group, count, jnp.int32(0))
        sums = stat_all[name]
        ratio = sums[2 * KVHEADS : 3 * KVHEADS, :used] / sums[KVHEADS : 2 * KVHEADS, :used]
        lane = lax.rem(lax.broadcasted_iota(jnp.int32, ratio.shape, 1), tail_rows)
        score_ref[d] = jnp.sum(jnp.where(lane == slot, ratio, 0.0))
    for t in range(bits):
        stat_copy(t).wait_send()

    @pl.loop(0, blocks)
    def _(j):
        for s in range(weight_steps):
            for copy in weight_copies(j, s):
                copy.wait_send()

    @pl.loop(0, pieces)
    def _(p):
        for s in range(pair_steps):
            for copy in pair_copies(p, s):
                copy.wait_send()
        for j in range(blocks - pair_blocks):
            context_copy(p, j).wait()


def fused(owners, picks, asks, block_lengths, store, queries, gain, wk, wv, wq, inverse, gains, bits, n_corpus):
    slots = n_corpus * CAP
    asking = queries.shape[1]
    tail_rows = pl.cdiv(slots, 16) * 16
    ask_rows = slots * asking
    pair_dev = owners.shape[0] // n_corpus // 2**bits
    pieces = slots // 2
    _, chunk, depth = store.shape
    own_rows = wq.shape[0]
    key_blocks = wk.shape[1] // WIDE
    pair_blocks = key_blocks + wv.shape[1] // WIDE
    blocks = pair_blocks + wq.shape[1] // WIDE
    held = slots * chunk
    total = held + tail_rows + ask_rows
    piece_rows = held // pieces
    stages = bits - 1
    cube = (2,) * bits
    lanes = pl.cdiv(GROUP * tail_rows, 128) * 128
    plan = (bits, slots, pieces, n_corpus, key_blocks, pair_blocks, blocks, n_corpus)
    whole = pl.BlockSpec(memory_space=pltpu.VMEM)
    apart = pl.BlockSpec(memory_space=pl.ANY)
    scalar = pl.BlockSpec(memory_space=pltpu.SMEM)
    return pl.pallas_call(
        functools.partial(gather_project_kernel, plan),
        out_shape=(
            jax.ShapeDtypeStruct((held, wq.shape[1]), store.dtype),
            jax.ShapeDtypeStruct((pair_dev,), jnp.float32),
        ),
        in_specs=[scalar] * 4 + [apart, apart, whole, apart, apart, apart, whole, whole],
        out_specs=(apart, scalar),
        scratch_shapes=[
            pltpu.SMEM((slots,), jnp.int32),
            pltpu.SMEM((slots,), jnp.int32),
            pltpu.SMEM((slots,), jnp.int32),
            pltpu.VMEM(store.shape, store.dtype),
            pltpu.VMEM(queries.shape, store.dtype),
            pltpu.VMEM((total, depth), store.dtype),
            pltpu.VMEM((blocks,) + cube + (own_rows, WIDE), store.dtype),
            pltpu.VMEM((blocks, total, WIDE), store.dtype),
            pltpu.VMEM((pieces,) + cube + (pair_blocks, piece_rows, WIDE), store.dtype),
            pltpu.VMEM((chunk, HDIM), jnp.float32),
            pltpu.VMEM((chunk, HDIM), jnp.float32),
            pltpu.VMEM((tail_rows + ask_rows, HDIM), jnp.float32),
            pltpu.VMEM((tail_rows + ask_rows, HDIM), jnp.float32),
            pltpu.VMEM((bits + 1, 8, lanes), jnp.float32),
            pltpu.VMEM((bits, 8, lanes), jnp.float32),
            pltpu.VMEM((n_corpus, 8, lanes), jnp.float32),
            pltpu.SemaphoreType.DMA((5,)),
            pltpu.SemaphoreType.DMA((blocks,)),
            pltpu.SemaphoreType.DMA((pieces,)),
            pltpu.SemaphoreType.DMA((bits + 2,)),
            pltpu.SemaphoreType.DMA((blocks + pieces, stages + 2, stages)),
            pltpu.SemaphoreType.DMA((blocks + pieces, stages + 2, stages)),
            pltpu.SemaphoreType.DMA((pieces, blocks - pair_blocks)),
            pltpu.SemaphoreType.DMA((2, bits + n_corpus + 1)),
        ],
        compiler_params=pltpu.CompilerParams(
            vmem_limit_bytes=VMEM, collective_id=0, has_side_effects=True
        ),
        cost_estimate=pl.CostEstimate(
            flops=2 * total * depth * blocks * WIDE,
            transcendentals=0,
            bytes_accessed=2 * (total * depth + depth * blocks * WIDE),
        ),
    )(owners, picks, asks, block_lengths, store, queries, gain, wk, wv, wq, inverse, gains)


def on_device(
    store_rows,
    block_lengths,
    queries,
    cand_owner,
    cand_block,
    cand_query,
    norm_gain,
    w_query,
    w_key,
    w_value,
    w_score,
):
    n_corpus = lax.axis_size("corpus")
    bits = lax.axis_size("rerank").bit_length() - 1
    half = HDIM // 2
    inverse = jnp.power(ROPE_BASE, -2.0 * jnp.arange(half, dtype=jnp.float32) / HDIM)
    inverse = jnp.concatenate([inverse, inverse])[None, :]
    context, scores = fused(
        cand_owner[:, 0],
        cand_block,
        cand_query,
        block_lengths,
        store_rows,
        queries,
        norm_gain,
        w_key,
        w_value,
        w_query,
        inverse,
        w_score.reshape(QHEADS, HDIM),
        bits,
        n_corpus,
    )
    return (context.reshape(n_corpus * CAP, store_rows.shape[1], context.shape[1]), scores)


def solution(mesh):
    placed = (
        P("corpus", "rerank", None),
        P(),
        P(None, "rerank", None),
        P(),
        P(),
        P(),
        P(),
        P("rerank", None),
        P("rerank", None),
        P("rerank", None),
        P(),
    )
    return jax.shard_map(
        on_device,
        mesh=mesh,
        in_specs=placed,
        out_specs=(P("corpus", "rerank", None), P(("corpus", "rerank"))),
        check_vma=False,
    )
```

```python
import functools

import jax
import jax.numpy as jnp
from jax import lax
from jax.experimental import pallas as pl
from jax.experimental.pallas import tpu as pltpu
from jax.sharding import PartitionSpec as P

HDIM = 128
QHEADS = 14
KVHEADS = 2
GROUP = QHEADS // KVHEADS
CAP = 5

ROPE_BASE = 1000000.0
EPSILON = 1e-06
NEG = -1e30
VMEM = 67043328


MESH = pl.DeviceIdType.MESH
WIDE = 2 * HDIM
DIRECT = 68
AHEAD = 2
WAIT = 3


def split_rows(rows, parts):
    unit = 16
    tiles = rows // unit
    sizes = [(tiles // parts + (p < tiles % parts)) * unit for p in range(parts)]
    starts = [sum(sizes[:p]) for p in range(parts)]
    return list(zip(starts, sizes))


def gather_project_kernel(
    plan,
    owner_ref,
    pick_ref,
    ask_ref,
    length_ref,
    store_hbm,
    query_hbm,
    gain_ref,
    wk_hbm,
    wv_hbm,
    wq_hbm,
    inverse_ref,
    gains_ref,
    out_hbm,
    score_ref,
    ids_ref,
    len_ref,
    query_ids,
    store,
    queries,
    normed,
    weight,
    result,
    pairs,
    pcos_ref,
    psin_ref,
    acos_ref,
    asin_ref,
    stat,
    stat_in,
    stat_all,
    load_sem,
    own_sem,
    put_sem,
    tail_sem,
    send_sem,
    recv_sem,
    out_sem,
    stat_sem,
):
    bits, slots, pieces, tiles, key_blocks, pair_blocks, blocks, n_corpus = plan
    member = lax.axis_index("rerank")
    corpus = lax.axis_index("corpus")
    shared = n_corpus % 2 == 0
    side = lax.rem(corpus, 2) if shared else 0
    mate = corpus + 1 - 2 * side
    links = list(range(1, bits))
    orders = [links[p:] + links[:p] for p in range(len(links))]
    stages = len(links)
    own_rows = wq_hbm.shape[0]
    chunk = store.shape[1]
    depth = store.shape[2]
    held = slots * chunk
    total = normed.shape[0]
    tail_rows = pl.cdiv(slots, 16) * 16
    piece_rows = held // pieces
    ask_rows = total - held - tail_rows

    def digit(b):
        return lax.rem(member // (2**b), 2)

    def across(b):
        return member + (1 - 2 * digit(b)) * (2**b)

    def place(spread):
        return tuple(slice(None) if b in spread else digit(b) for b in reversed(range(bits)))

    barrier = pltpu.get_barrier_semaphore()
    for b in range(bits):
        pl.semaphore_signal(
            barrier, inc=1, device_id={"rerank": across(b)}, device_id_type=MESH
        )
    for step in range(1, n_corpus):
        pl.semaphore_signal(
            barrier,
            inc=1,
            device_id={"corpus": lax.rem(corpus + step, n_corpus)},
            device_id_type=MESH,
        )

    own_copies = []
    for j in range(blocks):
        if j < key_blocks:
            source, column = wk_hbm, j
        elif j < pair_blocks:
            source, column = wv_hbm, j - key_blocks
        else:
            source, column = wq_hbm, j - pair_blocks
        own_copies.append(
            pltpu.make_async_copy(
                source.at[:, column * WIDE : (column + 1) * WIDE],
                weight.at[(j,) + place(())],
                own_sem.at[j],
            )
        )
        own_copies[-1].start()
    quarter = store.shape[0] // 4
    loads = [
        pltpu.make_async_copy(
            store_hbm.at[pl.ds(q * quarter, quarter)],
            store.at[pl.ds(q * quarter, quarter)],
            load_sem.at[q],
        )
        for q in range(4)
    ]
    loads.append(pltpu.make_async_copy(query_hbm, queries, load_sem.at[4]))
    for copy in loads:
        copy.start()
    pair_group = owner_ref.shape[0] // n_corpus

    @pl.loop(0, n_corpus)
    def _(g):
        def look(q, carry):
            count, picks, asks = carry
            p = g * pair_group + q
            mine = owner_ref[p] == corpus
            picks = tuple(
                jnp.where(mine & (count == r), pick_ref[p], v) for r, v in enumerate(picks)
            )
            asks = tuple(jnp.where(mine & (count == r), ask_ref[p], v) for r, v in enumerate(asks))
            return count + jnp.where(mine, 1, 0), picks, asks

        none = (jnp.int32(0),) * CAP
        count, picks, asks = lax.fori_loop(0, pair_group, look, (jnp.int32(0), none, none))
        for r in range(CAP):
            ids_ref[g * CAP + r] = picks[r]
            query_ids[g * CAP + r] = asks[r]
            length = length_ref[corpus * store.shape[0] + picks[r]]
            len_ref[g * CAP + r] = jnp.where(count > r, length, 0)

    pl.semaphore_wait(barrier, bits + n_corpus - 1)

    own_units = own_rows // 16
    direct = (own_units * DIRECT // 100) * 16 if shared else own_rows
    traded = own_rows - direct
    wparts = split_rows(direct, stages)
    kparts = split_rows(piece_rows, stages)

    def remote(ref, index, at, s, p, device):
        return pltpu.make_async_remote_copy(
            src_ref=ref.at[index],
            dst_ref=ref.at[index],
            send_sem=send_sem.at[at, s, p],
            recv_sem=recv_sem.at[at, s, p],
            device_id=device,
            device_id_type=MESH,
        )

    def weight_copies(block, s):
        out = []
        if s < stages:
            for p in range(stages):
                first, size = wparts[p]
                rows = pl.ds(pl.multiple_of(side * traded + first, 16), size)
                index = (block,) + place(orders[p][:s]) + (rows,)
                device = {"rerank": across(orders[p][s])}
                out.append(remote(weight, index, block, s, p, device))
        elif shared and s == stages:
            rows = pl.ds(pl.multiple_of(side * direct, 16), traded)
            for p in range(stages):
                spots = list(place(links[p + 1 :]))
                spots[bits - 1 - links[p]] = 1 - digit(links[p])
                index = (block,) + tuple(spots) + (rows,)
                out.append(remote(weight, index, block, s, p, {"corpus": mate}))
        else:
            index = (block,) + place(links)
            out.append(remote(weight, index, block, stages + 1, 0, {"rerank": across(0)}))
        return out

    def pair_copies(piece, s):
        out = []
        at = piece + blocks
        if s < stages:
            for p in range(stages):
                first, size = kparts[p]
                index = (piece,) + place(orders[p][:s]) + (slice(None), pl.ds(first, size))
                out.append(remote(pairs, index, at, s, p, {"rerank": across(orders[p][s])}))
        else:
            index = (piece,) + place(links)
            out.append(remote(pairs, index, at, stages + 1, 0, {"rerank": across(0)}))
        return out

    weight_steps = stages + 1 + shared
    pair_steps = stages + 1

    def own_pairs(piece):
        first = pl.multiple_of(piece * piece_rows, 16)
        return pltpu.make_async_copy(
            result.at[pl.ds(0, pair_blocks), pl.ds(first, piece_rows)],
            pairs.at[(piece,) + place(())],
            put_sem.at[piece],
        )

    def own_weight(block):
        return pltpu.make_async_copy(
            wq_hbm.at[:, :WIDE], weight.at[(block,) + place(())], own_sem.at[block]
        )

    def weight_event(e, block):
        if e == 0:
            own_weight(block).wait()
        else:
            for copy in weight_copies(block, e - 1):
                copy.wait_recv()
        if e < weight_steps:
            for copy in weight_copies(block, e):
                copy.start()

    def pair_event(e, piece):
        if e == 0:
            own_pairs(piece).wait()
        else:
            for copy in pair_copies(piece, e - 1):
                copy.wait_recv()
        if e < pair_steps:
            for copy in pair_copies(piece, e):
                copy.start()

    tail_order = links + [0]

    def ones(order):
        value = 1
        for b in order:
            value = value * digit(b)
        return value

    def tail_gets(t):
        return ones(tail_order[t + 1 :]) * (1 - digit(tail_order[t])) == 1

    def tail_gives(t):
        return ones(tail_order[t:]) == 1

    def tail_copy(t):
        return pltpu.make_async_remote_copy(
            src_ref=normed.at[held : held + tail_rows],
            dst_ref=normed.at[held : held + tail_rows],
            send_sem=tail_sem.at[1 + t],
            recv_sem=tail_sem.at[0],
            device_id={"rerank": across(tail_order[t])},
            device_id_type=MESH,
        )

    gain = gain_ref[...].astype(jnp.float32).reshape(1, depth)

    def scaled(rows):
        rows = rows.astype(jnp.float32)
        scale = lax.rsqrt(jnp.mean(rows * rows, axis=-1, keepdims=True) + EPSILON)
        return (rows * scale * gain).astype(normed.dtype)

    strip = 16

    def norm_slots(lo, hi):
        @pl.loop(lo, hi)
        def _(s):
            block = ids_ref[s]
            for r in range(chunk // strip):
                row = pl.multiple_of(s * chunk + r * strip, strip)
                normed[pl.ds(row, strip), :] = scaled(store[block, r * strip : (r + 1) * strip, :])

    lead = weight_steps
    cuts = [slots * i // lead for i in range(lead + 1)]

    asking = queries.shape[1]

    def asked_rows(s):
        return queries[query_ids[s]].astype(jnp.float32)

    def tables():
        def turn(positions):
            angles = positions.astype(jnp.float32) * inverse_ref[...]
            lane = lax.broadcasted_iota(jnp.int32, angles.shape, 1)
            sine = jnp.sin(angles)
            return jnp.cos(angles), jnp.where(lane < HDIM // 2, -sine, sine)

        here = lax.broadcasted_iota(jnp.int32, (chunk, HDIM), 0)
        pcos_ref[...], psin_ref[...] = turn(member * chunk + here)
        row = lax.broadcasted_iota(jnp.int32, (tail_rows, HDIM), 0)
        ends = jnp.zeros((tail_rows, HDIM), jnp.int32)
        row_asked = lax.broadcasted_iota(jnp.int32, (ask_rows, HDIM), 0)
        starts = member * asking + lax.rem(row_asked, asking)
        for s in range(slots):
            ends = jnp.where(row == s, len_ref[s] + (asking * 2**bits - 1), ends)
            starts = starts + jnp.where(row_asked // asking == s, len_ref[s], 0)
        acos_ref[:tail_rows], asin_ref[:tail_rows] = turn(ends)
        acos_ref[tail_rows:], asin_ref[tail_rows:] = turn(starts)

    for block in range(AHEAD):
        weight_event(0, block)
    for i in range(-lead, 0):
        for e in range(lead):
            block = i + lead - e + (AHEAD if e == 0 else 0)
            if block >= 0:
                weight_event(e, block)
        if i == -lead:
            tables()
            for copy in loads:
                copy.wait()

            @pl.when(ones(tail_order) == 1)
            def _():
                for r in range(tail_rows // strip):
                    rows = []
                    for s in range(r * strip, (r + 1) * strip):
                        rows.append(asked_rows(min(s, slots - 1))[asking - 1 :])
                    normed[held + r * strip : held + (r + 1) * strip, :] = jnp.concatenate(
                        rows, axis=0
                    ).astype(normed.dtype)

            @pl.loop(0, ask_rows // strip)
            def _(r):
                rows = pl.ds(pl.multiple_of(held + tail_rows + r * strip, strip), strip)
                each = strip // asking
                normed[rows, :] = scaled(
                    jnp.concatenate([asked_rows(r * each + k) for k in range(each)], axis=0)
                )

        norm_slots(cuts[i + lead], cuts[i + lead + 1])
        t = i + lead
        if t < bits:
            if t > 0:
                pl.when(tail_gets(t - 1))(lambda: tail_copy(t - 1).wait_recv())
            pl.when(tail_gives(t))(lambda: tail_copy(t).start())
    for t in range(min(lead, bits), bits):
        pl.when(tail_gets(t - 1))(lambda: tail_copy(t - 1).wait_recv())
        pl.when(tail_gives(t))(lambda: tail_copy(t).start())
    pl.when(tail_gets(bits - 1))(lambda: tail_copy(bits - 1).wait_recv())

    for t in range(bits):
        pl.when(tail_gives(t))(lambda: tail_copy(t).wait_send())
    for r in range(tail_rows // strip):
        rows = slice(held + r * strip, held + (r + 1) * strip)
        normed[rows, :] = scaled(normed[rows, :])

    tile_rows = held // tiles
    repeat = tile_rows // chunk

    def piece(block, start, rows, tail):
        x = normed[pl.ds(start, rows), :]
        w = weight[block].reshape(own_rows * 2**bits, WIDE)
        raw = jnp.dot(x, w, preferred_element_type=jnp.float32)
        plain = (block >= key_blocks) & (block < pair_blocks)

        def turn(part, cosine, sine):
            cosine = jnp.where(plain, 1.0, cosine)
            sine = jnp.where(plain, 0.0, sine)
            return part * cosine + pltpu.roll(part, HDIM // 2, 1) * sine

        for head in range(WIDE // HDIM):
            columns = slice(head * HDIM, (head + 1) * HDIM)
            for r in range(repeat):
                part = raw[r * chunk : (r + 1) * chunk, columns]
                result[block, pl.ds(start + r * chunk, chunk), columns] = turn(
                    part, pcos_ref[...], psin_ref[...]
                ).astype(result.dtype)
            if tail:
                result[block, held : held + tail, columns] = turn(
                    raw[tile_rows:, columns], acos_ref[:tail, :], asin_ref[:tail, :]
                ).astype(result.dtype)

    each = piece_rows // chunk
    scale = HDIM ** (-0.5)
    lanes = stat.shape[2]
    used = GROUP * tail_rows

    def spot(head):
        column = head * HDIM
        return column // WIDE, slice(column % WIDE, column % WIDE + HDIM)

    def tail_stats():
        rows = []
        for head in range(KVHEADS):
            parts = []
            for g in range(GROUP):
                block, columns = spot(head * GROUP + g)
                parts.append(result[pair_blocks + block, held : held + tail_rows, columns])
            query = jnp.concatenate(parts, axis=0)
            block, columns = spot(head)

            def both(block):
                return jnp.concatenate(
                    [result[block, :held, columns], result[block, held + tail_rows :, columns]],
                    axis=0,
                )

            key, value = both(block), both(key_blocks + block)
            slot = lax.rem(lax.broadcasted_iota(jnp.int32, (chunk, used), 1), tail_rows)
            token = member * chunk + lax.broadcasted_iota(jnp.int32, (chunk, used), 0)
            asked = ask_rows // slots
            slot_asked = lax.rem(lax.broadcasted_iota(jnp.int32, (asked, used), 1), tail_rows)

            def logits_of(lo, hi):
                return scale * lax.dot_general(
                    key[lo:hi], query, (((1,), (1,)), ((), ())), preferred_element_type=jnp.float32
                )

            seen = jnp.full((chunk, used), NEG, jnp.float32)
            for p in range(tiles):
                logits = logits_of(p * tile_rows, (p + 1) * tile_rows)
                for u in range(repeat):
                    s = p * repeat + u
                    alive = (slot == s) & (token < len_ref[s])
                    seen = jnp.where(alive, logits[u * chunk : (u + 1) * chunk], seen)
            logits = logits_of(held, held + ask_rows)
            asks = jnp.full((asked, used), NEG, jnp.float32)
            for s in range(slots):
                asks = jnp.where(slot_asked == s, logits[s * asked : (s + 1) * asked], asks)
            peak = jnp.maximum(
                jnp.max(seen, axis=0, keepdims=True), jnp.max(asks, axis=0, keepdims=True)
            )
            seen = jnp.exp(seen - peak)
            asks = jnp.exp(asks - peak)
            total = jnp.sum(seen, axis=0, keepdims=True) + jnp.sum(asks, axis=0, keepdims=True)
            spread = [
                jnp.where(slot == s, seen, 0.0).astype(jnp.bfloat16) for s in range(slots)
            ]
            spread.append(
                jnp.concatenate(
                    [jnp.where(slot_asked == s, asks, 0.0) for s in range(slots)], axis=0
                ).astype(jnp.bfloat16)
            )
            weighed = lax.dot_general(
                gains_ref[...], value, (((1,), (1,)), ((), ())), preferred_element_type=jnp.float32
            )
            mixed = jnp.dot(
                weighed.astype(jnp.bfloat16),
                jnp.concatenate(spread, axis=0),
                preferred_element_type=jnp.float32,
            )
            which = lax.broadcasted_iota(jnp.int32, mixed.shape, 0)
            wanted = head * GROUP + lax.broadcasted_iota(jnp.int32, mixed.shape, 1) // tail_rows
            part = jnp.sum(jnp.where(which == wanted, mixed, 0.0), axis=0, keepdims=True)
            rows.append((peak, total, part))
        stat[0] = jnp.zeros((8, lanes), jnp.float32)
        for k in range(3):
            for head in range(KVHEADS):
                row = k * KVHEADS + head
                stat[0, row : row + 1, :used] = rows[head][k]

    def stat_copy(t):
        return pltpu.make_async_remote_copy(
            src_ref=stat.at[t],
            dst_ref=stat_in.at[t],
            send_sem=stat_sem.at[0, t],
            recv_sem=stat_sem.at[1, t],
            device_id={"rerank": across(t)},
            device_id_type=MESH,
        )

    def score_copy(step):
        return pltpu.make_async_remote_copy(
            src_ref=stat.at[bits],
            dst_ref=stat_all.at[corpus],
            send_sem=stat_sem.at[0, bits + step],
            recv_sem=stat_sem.at[1, bits + step],
            device_id={"corpus": lax.rem(corpus + step, n_corpus)},
            device_id_type=MESH,
        )

    def score_own():
        return pltpu.make_async_copy(
            stat.at[bits], stat_all.at[corpus], stat_sem.at[0, bits + n_corpus]
        )

    def merge_stats():
        for t in range(bits):
            stat_copy(t).start()
            stat_copy(t).wait_recv()
            mine, other = stat[t], stat_in[t]

            def rows(values, k):
                return values[k * KVHEADS : (k + 1) * KVHEADS]

            peak = jnp.maximum(rows(mine, 0), rows(other, 0))
            left = jnp.exp(rows(mine, 0) - peak)
            right = jnp.exp(rows(other, 0) - peak)
            stat[t + 1] = jnp.zeros((8, lanes), jnp.float32)
            stat[t + 1, :KVHEADS] = peak
            for k in (1, 2):
                stat[t + 1, k * KVHEADS : (k + 1) * KVHEADS] = left * rows(mine, k) + right * rows(
                    other, k
                )
        for step in range(1, n_corpus):
            score_copy(step).start()
        score_own().start()

    def attend_slot(p, u, t):
        width = chunk * 2**t
        rows = pl.ds(pl.multiple_of(p * piece_rows + u * chunk, chunk), chunk)
        inner = pl.ds(pl.multiple_of(u * chunk, chunk), chunk)
        corner = (p,) + (0,) * (bits - t) + (slice(None),) * t
        token = member * chunk + lax.broadcasted_iota(jnp.int32, (chunk, width), 0)
        allowed = lax.broadcasted_iota(jnp.int32, (chunk, width), 1) <= token
        keep = member * chunk + lax.broadcasted_iota(jnp.int32, (chunk, HDIM), 0)
        keep = keep < len_ref[p * each + u]
        for head in range(KVHEADS):
            spots = [spot(head * GROUP + g) for g in range(GROUP)]
            query = jnp.concatenate(
                [result[pair_blocks + block, rows, columns] for block, columns in spots], axis=0
            )
            block, columns = spot(head)
            key = pairs[corner + (block, inner, columns)].reshape(width, HDIM)
            value = pairs[corner + (key_blocks + block, inner, columns)].reshape(width, HDIM)
            logits = lax.dot_general(
                query, key, (((1,), (1,)), ((), ())), preferred_element_type=jnp.float32
            ).reshape(GROUP, chunk, width)
            masked = jnp.where(allowed[None], logits, NEG)
            peak = jnp.max(masked, axis=-1, keepdims=True)
            weights = jnp.exp(scale * (masked - peak))
            inverse = 1.0 / jnp.sum(weights, axis=-1, keepdims=True)
            context = jnp.dot(
                weights.reshape(GROUP * chunk, width).astype(jnp.bfloat16),
                value,
                preferred_element_type=jnp.float32,
            )
            context = context.reshape(GROUP, chunk, HDIM) * inverse
            for g, (block, columns) in enumerate(spots):
                result[pair_blocks + block, rows, columns] = jnp.where(
                    keep, context[g], 0.0
                ).astype(result.dtype)

    def context_copy(p, j):
        rows = pl.ds(pl.multiple_of(p * piece_rows, 16), piece_rows)
        return pltpu.make_async_copy(
            result.at[pair_blocks + j, rows],
            out_hbm.at[rows, j * WIDE : (j + 1) * WIDE],
            out_sem.at[p, j],
        )

    def attend_piece(p):
        reach = [t for t in range(bits) if chunk * 2**t >= HDIM] + [bits]
        for k, t in enumerate(reach):
            low = 0 if k == 0 else 2 ** reach[k - 1]

            @pl.when((member >= low) & (member < 2**t))
            def _():
                @pl.loop(0, each)
                def _(u):
                    attend_slot(p, u, t)

        for j in range(blocks - pair_blocks):
            context_copy(p, j).start()

    begin = pair_blocks + WAIT
    finish = max(begin + pair_steps, blocks) + pieces

    @pl.loop(0, finish)
    def _(i):
        for e in range(weight_steps + 1):
            block = i + lead - e + (AHEAD if e == 0 else 0)

            @pl.when(block < blocks)
            def _():
                weight_event(e, block)

            if e <= pair_steps:
                part = i - begin - e

                @pl.when((part >= 0) & (part < pieces))
                def _():
                    pair_event(e, part)

        @pl.when(i < blocks)
        def _():
            @pl.loop(0, tiles - 1)
            def _(t):
                piece(i, pl.multiple_of(t * tile_rows, 16), tile_rows, 0)

        @pl.when(i < pair_blocks)
        def _():
            piece(i, held - tile_rows, tile_rows + tail_rows + ask_rows, tail_rows + ask_rows)

        @pl.when((i >= pair_blocks) & (i < blocks))
        def _():
            piece(i, held - tile_rows, tile_rows + tail_rows, tail_rows)

        @pl.when(i == pair_blocks - 1)
        def _():
            for p in range(pieces):
                own_pairs(p).start()

        @pl.when(i == blocks - 1)
        def _():
            tail_stats()

        @pl.when(i == blocks)
        def _():
            merge_stats()

        late = max(begin + pair_steps, blocks)
        done = i - late

        @pl.when((done >= 0) & (done < pieces))
        def _():
            attend_piece(done)

    for step in range(1, n_corpus):
        score_copy(step).wait()
    score_own().wait()
    pair_dev = pair_group // 2**bits
    first = corpus * pair_group
    for d in range(pair_dev):
        own = member * pair_dev + d
        name = owner_ref[first + own]

        def count(q, value):
            return value + jnp.where((owner_ref[first + q] == name) & (q < own), 1, 0)

        slot = corpus * CAP + lax.fori_loop(0, pair_group, count, jnp.int32(0))
        sums = stat_all[name]
        ratio = sums[2 * KVHEADS : 3 * KVHEADS, :used] / sums[KVHEADS : 2 * KVHEADS, :used]
        lane = lax.rem(lax.broadcasted_iota(jnp.int32, ratio.shape, 1), tail_rows)
        score_ref[d] = jnp.sum(jnp.where(lane == slot, ratio, 0.0))
    for t in range(bits):
        stat_copy(t).wait_send()

    @pl.loop(0, blocks)
    def _(j):
        for s in range(weight_steps):
            for copy in weight_copies(j, s):
                copy.wait_send()

    @pl.loop(0, pieces)
    def _(p):
        for s in range(pair_steps):
            for copy in pair_copies(p, s):
                copy.wait_send()
        for j in range(blocks - pair_blocks):
            context_copy(p, j).wait()


def fused(owners, picks, asks, block_lengths, store, queries, gain, wk, wv, wq, inverse, gains, bits, n_corpus):
    slots = n_corpus * CAP
    asking = queries.shape[1]
    tail_rows = pl.cdiv(slots, 16) * 16
    ask_rows = slots * asking
    pair_dev = owners.shape[0] // n_corpus // 2**bits
    pieces = slots // 2
    _, chunk, depth = store.shape
    own_rows = wq.shape[0]
    key_blocks = wk.shape[1] // WIDE
    pair_blocks = key_blocks + wv.shape[1] // WIDE
    blocks = pair_blocks + wq.shape[1] // WIDE
    held = slots * chunk
    total = held + tail_rows + ask_rows
    piece_rows = held // pieces
    stages = bits - 1
    cube = (2,) * bits
    lanes = pl.cdiv(GROUP * tail_rows, 128) * 128
    plan = (bits, slots, pieces, n_corpus, key_blocks, pair_blocks, blocks, n_corpus)
    whole = pl.BlockSpec(memory_space=pltpu.VMEM)
    apart = pl.BlockSpec(memory_space=pl.ANY)
    scalar = pl.BlockSpec(memory_space=pltpu.SMEM)
    return pl.pallas_call(
        functools.partial(gather_project_kernel, plan),
        out_shape=(
            jax.ShapeDtypeStruct((held, wq.shape[1]), store.dtype),
            jax.ShapeDtypeStruct((pair_dev,), jnp.float32),
        ),
        in_specs=[scalar] * 4 + [apart, apart, whole, apart, apart, apart, whole, whole],
        out_specs=(apart, scalar),
        scratch_shapes=[
            pltpu.SMEM((slots,), jnp.int32),
            pltpu.SMEM((slots,), jnp.int32),
            pltpu.SMEM((slots,), jnp.int32),
            pltpu.VMEM(store.shape, store.dtype),
            pltpu.VMEM(queries.shape, store.dtype),
            pltpu.VMEM((total, depth), store.dtype),
            pltpu.VMEM((blocks,) + cube + (own_rows, WIDE), store.dtype),
            pltpu.VMEM((blocks, total, WIDE), store.dtype),
            pltpu.VMEM((pieces,) + cube + (pair_blocks, piece_rows, WIDE), store.dtype),
            pltpu.VMEM((chunk, HDIM), jnp.float32),
            pltpu.VMEM((chunk, HDIM), jnp.float32),
            pltpu.VMEM((tail_rows + ask_rows, HDIM), jnp.float32),
            pltpu.VMEM((tail_rows + ask_rows, HDIM), jnp.float32),
            pltpu.VMEM((bits + 1, 8, lanes), jnp.float32),
            pltpu.VMEM((bits, 8, lanes), jnp.float32),
            pltpu.VMEM((n_corpus, 8, lanes), jnp.float32),
            pltpu.SemaphoreType.DMA((5,)),
            pltpu.SemaphoreType.DMA((blocks,)),
            pltpu.SemaphoreType.DMA((pieces,)),
            pltpu.SemaphoreType.DMA((bits + 2,)),
            pltpu.SemaphoreType.DMA((blocks + pieces, stages + 2, stages)),
            pltpu.SemaphoreType.DMA((blocks + pieces, stages + 2, stages)),
            pltpu.SemaphoreType.DMA((pieces, blocks - pair_blocks)),
            pltpu.SemaphoreType.DMA((2, bits + n_corpus + 1)),
        ],
        compiler_params=pltpu.CompilerParams(
            vmem_limit_bytes=VMEM, collective_id=0, has_side_effects=True
        ),
        cost_estimate=pl.CostEstimate(
            flops=2 * total * depth * blocks * WIDE,
            transcendentals=0,
            bytes_accessed=2 * (total * depth + depth * blocks * WIDE),
        ),
    )(owners, picks, asks, block_lengths, store, queries, gain, wk, wv, wq, inverse, gains)


def hand_over_kernel(parts, source, target, held, in_sem, out_sem):
    rows = source.shape[0] // parts

    def copies(c):
        span = pl.ds(c * rows, rows)
        return (
            pltpu.make_async_copy(source.at[span], held.at[span], in_sem.at[c]),
            pltpu.make_async_copy(held.at[span], target.at[span], out_sem.at[c]),
        )

    for c in range(parts):
        copies(c)[0].start()
    for c in range(parts):
        taken, put = copies(c)
        taken.wait()
        put.start()
    for c in range(parts):
        copies(c)[1].wait()


def hand_over(values, parts):
    apart = pl.BlockSpec(memory_space=pl.ANY)
    return pl.pallas_call(
        functools.partial(hand_over_kernel, parts),
        out_shape=jax.ShapeDtypeStruct(values.shape, values.dtype),
        in_specs=[apart],
        out_specs=apart,
        scratch_shapes=[
            pltpu.VMEM(values.shape, values.dtype),
            pltpu.SemaphoreType.DMA((parts,)),
            pltpu.SemaphoreType.DMA((parts,)),
        ],
        compiler_params=pltpu.CompilerParams(vmem_limit_bytes=VMEM),
    )(values)


def on_device(
    store_rows,
    block_lengths,
    queries,
    cand_owner,
    cand_block,
    cand_query,
    norm_gain,
    w_query,
    w_key,
    w_value,
    w_score,
):
    n_corpus = lax.axis_size("corpus")
    bits = lax.axis_size("rerank").bit_length() - 1
    half = HDIM // 2
    inverse = jnp.power(ROPE_BASE, -2.0 * jnp.arange(half, dtype=jnp.float32) / HDIM)
    inverse = jnp.concatenate([inverse, inverse])[None, :]
    context, scores = fused(
        cand_owner[:, 0],
        cand_block,
        cand_query,
        block_lengths,
        store_rows,
        queries,
        norm_gain,
        w_key,
        w_value,
        w_query,
        inverse,
        w_score.reshape(QHEADS, HDIM),
        bits,
        n_corpus,
    )
    context = hand_over(context, n_corpus * CAP // 2)
    return (context.reshape(n_corpus * CAP, store_rows.shape[1], context.shape[1]), scores)


def solution(mesh):
    placed = (
        P("corpus", "rerank", None),
        P(),
        P(None, "rerank", None),
        P(),
        P(),
        P(),
        P(),
        P("rerank", None),
        P("rerank", None),
        P("rerank", None),
        P(),
    )
    return jax.shard_map(
        on_device,
        mesh=mesh,
        in_specs=placed,
        out_specs=(P("corpus", "rerank", None), P(("corpus", "rerank"))),
        check_vma=False,
    )
```
